32 devices in a mesh: lat: 8 (over y, x, core), lon: 4 (over z).
Axes of the slice: x: 2, y: 2, z: 4, core: 2. Of those that a mesh axis runs over, the one named last changes fastest.
Arguments:
- obs_frac: float32 [8, 4, 2, 1024], P('lat', 'lon'), may hold values from 0 to 1
- obs_field: float32 [8, 4, 3, 1024], P('lat', 'lon'), may hold values from -6 to 6
- dipole_frac: float32 [8, 4, 2, 256], P('lat', 'lon'), may hold values from 0 to 1
- dipole_moment: float32 [8, 4, 256], P('lat', 'lon'), may hold values from -6 to 6
- obs_count: int32 [8, 4], P('lat', 'lon'), may hold values from 256 to 1024, as said below
Outputs:
- gram: float32 [8, 4, 13, 256, 256], P('lat', 'lon')
- rhs: float32 [8, 4, 256], P('lat', 'lon')
The draws below stay inside these ranges and needn't reach their ends.
Inputs may be any that keep to these rules, and one draw needn't show every extreme that they name: `obs_count`: tiles of the first and of the last latitude row hold exactly 1024 observations; every other tile holds between 256 and 512.
All inputs are finite; a program needn't handle non-finite values.
Results may differ from the reference program's by a relative error of at most 0.0003.
Values sent between devices are 32-bit elements; how exact they have to be, the bound alone decides.
No kernel may reach another device: no remote copies, remote signals or barrier semaphores. Data moves between devices by JAX's collectives and lax.ppermute only.
A program may use at most 128 MiB of HBM per device.

```python
import math
import jax
import jax.numpy as jnp
from jax import lax

BS = 256
OBS = 1024
LAT_TILES = 8
LON_TILES = 4


def draw_obs_count(key, part):
    middle = jax.random.randint(key, (LAT_TILES, LON_TILES), OBS // 4, OBS // 2 + 1)
    lat_rows = jnp.arange(LAT_TILES)[:, None] + jnp.zeros((LAT_TILES, LON_TILES), jnp.int32)
    polar = (lat_rows == 0) | (lat_rows == LAT_TILES - 1)
    return jnp.where(polar, OBS, middle).astype(jnp.int32)


def block_levels(stream_key, dims, shards, low, top_value):
    level = 1.0
    for axis_at, shards_of in shards:
        draws = jax.random.uniform(jax.random.fold_in(jax.random.fold_in(stream_key, 6), axis_at), (shards_of,), jnp.float32, low / len(shards), top_value / len(shards))
        level = level * jnp.repeat(jnp.exp(draws), dims[axis_at] // shards_of).reshape((-1,) + (1,) * (len(dims) - 1 - axis_at))
    return level


def normal_values(stream_key, shape, spread, limit, cuts=(), kind=jnp.bfloat16):
    factor_of = block_levels(stream_key, shape, cuts, -0.22, 0.18) if cuts else 1.0
    array = jax.random.normal(stream_key, shape, jnp.float32) * spread * factor_of
    return jnp.minimum(jnp.maximum(array, -limit), limit).astype(kind)


def setup_inputs(seed: int = 0) -> dict:
    seeds = jax.random.split(jax.random.key(seed), 6)
    return {
        "obs_frac": jnp.clip(1.0 * jax.random.uniform(seeds[0], (LAT_TILES, LON_TILES, 2, OBS), jnp.float32) ** block_levels(seeds[0], (LAT_TILES, LON_TILES, 2, OBS), ((0, 8), (1, 4)), -0.2, 0.2), 0.0, 1.0),
        "obs_field": normal_values(seeds[1], (LAT_TILES, LON_TILES, 3, OBS), 1.0, 6.0, ((0, 8), (1, 4)), jnp.float32),
        "dipole_frac": jnp.clip(1.0 * jax.random.uniform(seeds[2], (LAT_TILES, LON_TILES, 2, BS), jnp.float32) ** block_levels(seeds[2], (LAT_TILES, LON_TILES, 2, BS), ((0, 8), (1, 4)), -0.2, 0.2), 0.0, 1.0),
        "dipole_moment": normal_values(seeds[3], (LAT_TILES, LON_TILES, BS), 1.0, 6.0, ((0, 8), (1, 4)), jnp.float32),
        "obs_count": draw_obs_count(jax.random.fold_in(seeds[5], 71), 0),
    }


CROSS = ((0, 0), (-1, 0), (1, 0), (0, -1), (0, 1))
OFFSETS = ((0, 0), (-1, 0), (1, 0), (0, -1), (0, 1), (-2, 0), (2, 0), (0, -2), (0, 2), (-1, -1), (-1, 1), (1, -1), (1, 1))
OBS_RADIUS = 1.06
SOURCE_RADIUS = 0.99
KERNEL_SCALE = 1e-4
HUBER_EDGE = 0.8
DEGREE = math.pi / 180.0


def place(fraction, lat_index, lon_index, lat_tiles, lon_tiles, radius):
    lat_span = 160.0 * DEGREE / lat_tiles
    latitude = -80.0 * DEGREE + (lat_index + fraction[0]) * lat_span
    longitude = (lon_index + fraction[1]) * (2.0 * math.pi / lon_tiles)
    return radius * jnp.stack([jnp.cos(latitude) * jnp.cos(longitude), jnp.cos(latitude) * jnp.sin(longitude), jnp.sin(latitude)])


def kernel(points, sources):
    separation = points[:, :, None] - sources[:, None, :]
    squared = jnp.sum(separation * separation, axis=0)
    aligned = jnp.sum(sources[:, None, :] * separation, axis=0)
    inverse_cube = squared ** -1.5
    return KERNEL_SCALE * (3.0 * aligned / squared * separation - sources[:, None, :]) * inverse_cube


def moved(tiles_block, lat_step, lon_step):
    tiles_block = jnp.roll(tiles_block, lon_step, axis=1)
    if lat_step == 1:
        tiles_block = jnp.concatenate([jnp.zeros_like(tiles_block[:1]), tiles_block[:-1]], 0)
    elif lat_step == -1:
        tiles_block = jnp.concatenate([tiles_block[1:], jnp.zeros_like(tiles_block[:1])], 0)
    return tiles_block


def reference(obs_frac, obs_field, dipole_frac, dipole_moment, obs_count):
    lat_ids = jnp.arange(LAT_TILES, dtype=jnp.int32)
    lon_ids = jnp.arange(LON_TILES, dtype=jnp.int32)

    def place_row(fractions, lat_index):
        return jax.vmap(lambda member, lon_index: place(member, lat_index, lon_index, LAT_TILES, LON_TILES, SOURCE_RADIUS))(fractions, lon_ids)

    sources_all = jax.vmap(place_row)(dipole_frac, lat_ids)
    zero_row = jnp.zeros_like(sources_all[:1])
    sources_pad = jnp.concatenate([zero_row, sources_all, zero_row], 0)
    zero_moment = jnp.zeros_like(dipole_moment[:1])
    moments_pad = jnp.concatenate([zero_moment, dipole_moment, zero_moment], 0)

    def tile_work(tile_number):
        lat_row = tile_number // LON_TILES
        lon_col = tile_number % LON_TILES
        source_list = []
        moment_list = []
        for lat_step, lon_step in CROSS:
            source_list.append(sources_pad[lat_row + 1 + lat_step, (lon_col + lon_step) % LON_TILES])
            moment_list.append(moments_pad[lat_row + 1 + lat_step, (lon_col + lon_step) % LON_TILES])
        sources = jnp.concatenate(source_list, 1)
        moments = jnp.concatenate(moment_list, 0)
        points = place(obs_frac[lat_row, lon_col], lat_row, lon_col, LAT_TILES, LON_TILES, OBS_RADIUS)
        coupling = kernel(points, sources)
        predicted = jnp.einsum('coj,j->co', coupling, moments, precision=lax.Precision.HIGHEST)
        residual = obs_field[lat_row, lon_col] - predicted
        present = (jnp.arange(OBS, dtype=jnp.int32) < obs_count[lat_row, lon_col]).astype(jnp.float32)
        weight = present * HUBER_EDGE / jnp.maximum(jnp.abs(residual), HUBER_EDGE)
        coupling_low = coupling.astype(jnp.bfloat16)
        weighted_low = (weight[:, :, None] * coupling).astype(jnp.bfloat16)
        partial_value = jnp.einsum('coi,coj->ij', weighted_low.astype(jnp.float32), coupling_low.astype(jnp.float32), precision=lax.Precision.HIGHEST)
        right_side = jnp.einsum('coi,co->i', coupling, weight * residual, precision=lax.Precision.HIGHEST)
        return partial_value, right_side

    partials, rights = lax.map(tile_work, jnp.arange(LAT_TILES * LON_TILES, dtype=jnp.int32))
    pair_blocks = partials.reshape(LAT_TILES, LON_TILES, 5, BS, 5, BS)
    right_blocks = rights.reshape(LAT_TILES, LON_TILES, 5, BS)
    blocks = [jnp.zeros((LAT_TILES, LON_TILES, BS, BS), jnp.float32) for offset in OFFSETS]
    rhs = jnp.zeros((LAT_TILES, LON_TILES, BS), jnp.float32)
    for first, (lat_step, lon_step) in enumerate(CROSS):
        rhs = rhs + moved(right_blocks[:, :, first], lat_step, lon_step)
        for second, (lat_other, lon_other) in enumerate(CROSS):
            target = OFFSETS.index((lat_other - lat_step, lon_other - lon_step))
            blocks[target] = blocks[target] + moved(pair_blocks[:, :, first, :, second, :], lat_step, lon_step)
    gram = jnp.stack(blocks, axis=2)
    return gram, rhs
```

```python
import functools
import math

import jax
import jax.numpy as jnp
from jax import lax
from jax.experimental import pallas as pl
from jax.experimental.pallas import tpu as pltpu
from jax.sharding import PartitionSpec as P

CROSS = ((0, 0), (-1, 0), (1, 0), (0, -1), (0, 1))
OFFSETS = (
    (0, 0),
    (-1, 0),
    (1, 0),
    (0, -1),
    (0, 1),
    (-2, 0),
    (2, 0),
    (0, -2),
    (0, 2),
    (-1, -1),
    (-1, 1),
    (1, -1),
    (1, 1),
)
OBS_RADIUS = 1.06
SOURCE_RADIUS = 0.99
KERNEL_SCALE = 0.0001
HUBER_EDGE = 0.8
DEGREE = math.pi / 180.0
CHUNK = 256
ROWS = 16
LANES = 128


def cycled(value, axis, steps):
    count = lax.axis_size(axis)
    return lax.ppermute(value, axis, [(i, (i + steps) % count) for i in range(count)])


def place(fraction, lat_index, lon_index, lat_tiles, lon_tiles, radius):
    lat_span = 160.0 * DEGREE / lat_tiles
    latitude = -80.0 * DEGREE + (lat_index + fraction[0]) * lat_span
    longitude = (lon_index + fraction[1]) * (2.0 * math.pi / lon_tiles)
    return radius * jnp.stack(
        [
            jnp.cos(latitude) * jnp.cos(longitude),
            jnp.cos(latitude) * jnp.sin(longitude),
            jnp.sin(latitude),
        ]
    )


def row_kernel(
    own_ref,
    north_ref,
    south_ref,
    west_ref,
    east_ref,
    far_north_ref,
    far_south_ref,
    far_west_ref,
    far_east_ref,
    gram_ref,
    rhs_ref,
    obs,
    column,
    held_even,
    held_odd,
    weighted_even,
    weighted_odd,
    kept,
    predicted,
    right,
    table,
    items,
    members,
    *,
    lat_tiles,
):
    size = rhs_ref.shape[1]
    chunks = obs.shape[0] // len(CROSS)
    slots = chunks * CHUNK
    lat = lax.axis_index("lat")

    for tile, ref in enumerate((own_ref, north_ref, south_ref, west_ref, east_ref)):
        for chunk in range(chunks):
            obs[tile * chunks + chunk] = ref[:, chunk * CHUNK : (chunk + 1) * CHUNK]
    sources = {(0, 0): own_ref, (-1, 0): north_ref, (1, 0): south_ref, (0, -1): west_ref, (0, 1): east_ref}
    sources = {offset: (ref, slots) for offset, ref in sources.items()}
    for at, offset in enumerate(((-2, 0), (-1, -1), (-1, 1))):
        sources[offset] = (far_north_ref, at * size)
    for at, offset in enumerate(((2, 0), (1, -1), (1, 1))):
        sources[offset] = (far_south_ref, at * size)
    sources[(0, -2)] = (far_west_ref, 0)
    sources[(0, 2)] = (far_east_ref, 0)

    def inside(step):
        return (lat + step >= 0) & (lat + step < lat_tiles)

    for target, offset in enumerate(OFFSETS):
        ref, start = sources[offset]
        upright = ref[:, start : start + size].T
        for part in range(4):
            values = jnp.broadcast_to(upright[:, part : part + 1], (size, LANES))
            if part == 3 and offset[0] != 0:
                values = values * inside(offset[0]).astype(jnp.float32)
            column[target, part] = values

    total = jnp.int32(0)
    for tile in (0, 3, 4, 1, 2):
        step = CROSS[tile]
        row = lat + step[0]
        first_row, last_row = row == 0, row == lat_tiles - 1
        own = (-step[0], -step[1])
        rest = [b for b in CROSS if b != own and b[0] == 0]
        ends = [b for b in CROSS if b != own and b[0] != 0]
        order = [OFFSETS.index((b[0] + step[0], b[1] + step[1])) for b in [own] + rest + ends]
        for at, target in enumerate(order):
            table[tile, at] = target
        if len(ends) == 2:
            table[tile, 3] = jnp.where(first_row, order[4], order[3])
            table[tile, 4] = jnp.where(first_row, order[3], order[4])
        members[tile] = 5 - first_row.astype(jnp.int32) - last_row.astype(jnp.int32)
        count = jnp.where(first_row | last_row, chunks, chunks // 2)
        count = jnp.where(inside(step[0]), count, 0)

        def note(chunk, at, tile=tile):
            items[0, at] = tile
            items[1, at] = tile * chunks + chunk
            return at + 1

        total = lax.fori_loop(0, count, note, total)

    gram_ref[...] = jnp.zeros_like(gram_ref)
    held_odd[...] = jnp.zeros_like(held_odd)
    weighted_odd[...] = jnp.zeros_like(weighted_odd)
    right[...] = jnp.zeros_like(right)

    def evaluate(tile, chunk, at, held):
        target = table[tile, at]
        spare = (at != 0).astype(jnp.int32)
        point = [jnp.broadcast_to(obs[chunk, c : c + 1, :], (ROWS, CHUNK)) for c in range(3)]
        sums = [predicted[c] for c in range(3)]
        near = 3.0 * (OBS_RADIUS * OBS_RADIUS - SOURCE_RADIUS * SOURCE_RADIUS) * 0.5 * KERNEL_SCALE
        for start in range(0, size, ROWS):
            span = slice(start, start + ROWS)
            wide = [jnp.concatenate([column[target, part, span, :]] * (CHUNK // LANES), axis=1) for part in range(4)]
            apart = [point[c] - wide[c] for c in range(3)]
            squared = apart[0] * apart[0] + apart[1] * apart[1] + apart[2] * apart[2]
            inverse = lax.rsqrt(squared)
            inverse_square = inverse * inverse
            cube = inverse_square * inverse
            along = cube * (near * inverse_square - 1.5 * KERNEL_SCALE)
            across = cube * KERNEL_SCALE
            for c in range(3):
                value = along * apart[c] - across * wide[c]
                held[at, span, c * CHUNK : (c + 1) * CHUNK] = value.astype(jnp.bfloat16)
                kept[spare, c, span, :] = value
                part = value * wide[3]
                for sub in range(0, ROWS, 8):
                    sums[c] = sums[c] + part[sub : sub + 8]
        for c in range(3):
            predicted[c] = sums[c]

    def multiply(tile, at, held, weighted):
        target = table[tile, at]
        gram_ref[target] += lax.dot_general(
            weighted[...], held[at], (((1,), (1,)), ((), ())), preferred_element_type=jnp.float32
        )

    def finish(chunk, weighted):
        present = obs[chunk, 6:7, :]
        scale, force = [], []
        for c in range(3):
            residual = obs[chunk, 3 + c : 4 + c, :] - jnp.sum(predicted[c], axis=0, keepdims=True)
            weight = present * HUBER_EDGE / jnp.maximum(jnp.abs(residual), HUBER_EDGE)
            scale.append(jnp.broadcast_to(weight, (ROWS, CHUNK)))
            force.append(jnp.broadcast_to(weight * residual, (ROWS, CHUNK)))
        for start in range(0, size, ROWS):
            span = slice(start, start + ROWS)
            pull = None
            for c in range(3):
                value = kept[0, c, span, :]
                weighted[span, c * CHUNK : (c + 1) * CHUNK] = (scale[c] * value).astype(jnp.bfloat16)
                part = force[c] * value
                pull = part if pull is None else pull + part
            for lane in range(0, CHUNK, LANES):
                right[span, :] += pull[:, lane : lane + LANES]

    def advance(item, held, weighted, held_before, weighted_before):
        tile, chunk = items[0, item], items[1, item]
        before = items[0, jnp.maximum(item - 1, 0)]
        predicted[...] = jnp.zeros_like(predicted)

        def block(at, carry):
            multiply(before, at, held_before, weighted_before)
            evaluate(tile, chunk, at, held)
            return carry

        lax.fori_loop(0, jnp.maximum(members[tile], members[before]), block, 0)
        finish(chunk, weighted)

    def pair(at, carry):
        advance(2 * at, held_even, weighted_even, held_odd, weighted_odd)
        advance(2 * at + 1, held_odd, weighted_odd, held_even, weighted_even)
        return carry

    lax.fori_loop(0, total // 2, pair, 0)
    last = items[0, total - 1]

    def drain(at, carry):
        multiply(last, at, held_odd, weighted_odd)
        return carry

    lax.fori_loop(0, members[last], drain, 0)

    for target, offset in enumerate(OFFSETS):
        if offset[0] != 0:

            @pl.when(jnp.logical_not(inside(offset[0])))
            def _():
                gram_ref[target] = jnp.zeros_like(gram_ref[target])

    rhs_ref[...] = jnp.sum(right[...].T, axis=0, keepdims=True)


def shards(obs_frac, obs_field, dipole_frac, dipole_moment, obs_count):
    lat_tiles = lax.axis_size("lat")
    lon_tiles = lax.axis_size("lon")
    lat_index = lax.axis_index("lat")
    lon_index = lax.axis_index("lon")
    size = dipole_frac.shape[3]
    slots = obs_frac.shape[3]
    source = place(dipole_frac[0, 0], lat_index, lon_index, lat_tiles, lon_tiles, SOURCE_RADIUS)
    points = place(obs_frac[0, 0], lat_index, lon_index, lat_tiles, lon_tiles, OBS_RADIUS)
    present = (jnp.arange(slots, dtype=jnp.int32) < obs_count[0, 0]).astype(jnp.float32)
    observed = jnp.concatenate([points, obs_field[0, 0], present[None], jnp.zeros((1, slots), jnp.float32)], 0)
    dipoles = jnp.concatenate([source, dipole_moment[0, 0][None], jnp.zeros((4, size), jnp.float32)], 0)
    package = jnp.concatenate([observed, dipoles], 1)
    north = cycled(package, "lat", 1)
    south = cycled(package, "lat", -1)
    west = cycled(package, "lon", 1)
    east = cycled(package, "lon", -1)
    far_north = cycled(jnp.concatenate([north[:, slots:], west[:, slots:], east[:, slots:]], 1), "lat", 1)
    far_south = cycled(jnp.concatenate([south[:, slots:], west[:, slots:], east[:, slots:]], 1), "lat", -1)
    far_west = cycled(west[:, slots:], "lon", 1)
    far_east = cycled(east[:, slots:], "lon", -1)
    chunks = slots // CHUNK
    gram, rhs = pl.pallas_call(
        functools.partial(row_kernel, lat_tiles=lat_tiles),
        out_shape=(
            jax.ShapeDtypeStruct((len(OFFSETS), size, size), jnp.float32),
            jax.ShapeDtypeStruct((1, size), jnp.float32),
        ),
        in_specs=[pl.BlockSpec(memory_space=pltpu.VMEM)] * 9,
        out_specs=(pl.BlockSpec(memory_space=pltpu.VMEM), pl.BlockSpec(memory_space=pltpu.VMEM)),
        scratch_shapes=[
            pltpu.VMEM((5 * chunks, 8, CHUNK), jnp.float32),
            pltpu.VMEM((len(OFFSETS), 4, size, LANES), jnp.float32),
            pltpu.VMEM((5, size, 3 * CHUNK), jnp.bfloat16),
            pltpu.VMEM((5, size, 3 * CHUNK), jnp.bfloat16),
            pltpu.VMEM((size, 3 * CHUNK), jnp.bfloat16),
            pltpu.VMEM((size, 3 * CHUNK), jnp.bfloat16),
            pltpu.VMEM((2, 3, size, CHUNK), jnp.float32),
            pltpu.VMEM((3, 8, CHUNK), jnp.float32),
            pltpu.VMEM((size, LANES), jnp.float32),
            pltpu.SMEM((5, 5), jnp.int32),
            pltpu.SMEM((2, 5 * chunks), jnp.int32),
            pltpu.SMEM((5,), jnp.int32),
        ],
        compiler_params=pltpu.CompilerParams(vmem_limit_bytes=60 * 1024 * 1024),
        name="row_blocks",
    )(package, north, south, west, east, far_north, far_south, far_west, far_east)
    return (gram[None, None], rhs[None])


def solution(mesh):
    in_specs = (
        P("lat", "lon", None, None),
        P("lat", "lon", None, None),
        P("lat", "lon", None, None),
        P("lat", "lon", None),
        P("lat", "lon"),
    )
    out_specs = (P("lat", "lon", None, None, None), P("lat", "lon", None))
    return jax.shard_map(shards, mesh=mesh, in_specs=in_specs, out_specs=out_specs, check_vma=False)
```

```python
import functools
import math

import jax
import jax.numpy as jnp
from jax import lax
from jax.experimental import pallas as pl
from jax.experimental.pallas import tpu as pltpu
from jax.sharding import PartitionSpec as P

CROSS = ((0, 0), (-1, 0), (1, 0), (0, -1), (0, 1))
OFFSETS = (
    (0, 0),
    (-1, 0),
    (1, 0),
    (0, -1),
    (0, 1),
    (-2, 0),
    (2, 0),
    (0, -2),
    (0, 2),
    (-1, -1),
    (-1, 1),
    (1, -1),
    (1, 1),
)
OBS_RADIUS = 1.06
SOURCE_RADIUS = 0.99
KERNEL_SCALE = 0.0001
HUBER_EDGE = 0.8
DEGREE = math.pi / 180.0
CHUNK = 256
ROWS = 16
LANES = 128
DEPTH = 64
STRETCH = KERNEL_SCALE ** (-2.0 / 3.0)


def cycled(value, axis, steps):
    count = lax.axis_size(axis)
    return lax.ppermute(value, axis, [(i, (i + steps) % count) for i in range(count)])


def place(fraction, lat_index, lon_index, lat_tiles, lon_tiles, radius):
    lat_span = 160.0 * DEGREE / lat_tiles
    latitude = -80.0 * DEGREE + (lat_index + fraction[0]) * lat_span
    longitude = (lon_index + fraction[1]) * (2.0 * math.pi / lon_tiles)
    return radius * jnp.stack(
        [
            jnp.cos(latitude) * jnp.cos(longitude),
            jnp.cos(latitude) * jnp.sin(longitude),
            jnp.sin(latitude),
        ]
    )


def split(values):
    high = values.astype(jnp.bfloat16).astype(jnp.float32)
    rest = values - high
    middle = rest.astype(jnp.bfloat16).astype(jnp.float32)
    return high, middle, rest - middle


def row_kernel(
    own_ref,
    north_ref,
    south_ref,
    west_ref,
    east_ref,
    far_north_ref,
    far_south_ref,
    far_west_ref,
    far_east_ref,
    gram_ref,
    rhs_ref,
    obs,
    column,
    tall,
    flat,
    held_even,
    held_odd,
    weighted_even,
    weighted_odd,
    apart_even,
    apart_odd,
    kept,
    predicted,
    right,
    table,
    items,
    members,
    counts,
    *,
    lat_tiles,
):
    size = rhs_ref.shape[1]
    chunks = obs.shape[0] // len(CROSS)
    slots = chunks * CHUNK
    lat = lax.axis_index("lat")

    for tile, ref in enumerate((own_ref, north_ref, south_ref, west_ref, east_ref)):
        for chunk in range(chunks):
            obs[tile * chunks + chunk] = ref[:, chunk * CHUNK : (chunk + 1) * CHUNK]
    sources = {(0, 0): own_ref, (-1, 0): north_ref, (1, 0): south_ref, (0, -1): west_ref, (0, 1): east_ref}
    sources = {offset: (ref, slots) for offset, ref in sources.items()}
    for at, offset in enumerate(((-2, 0), (-1, -1), (-1, 1))):
        sources[offset] = (far_north_ref, at * size)
    for at, offset in enumerate(((2, 0), (1, -1), (1, 1))):
        sources[offset] = (far_south_ref, at * size)
    sources[(0, -2)] = (far_west_ref, 0)
    sources[(0, 2)] = (far_east_ref, 0)

    def inside(step):
        return (lat + step >= 0) & (lat + step < lat_tiles)

    picks = lax.broadcasted_iota(jnp.int32, (DEPTH, 4 * LANES), 0)
    parts = lax.broadcasted_iota(jnp.int32, (DEPTH, 4 * LANES), 1) // LANES
    picks = ((picks == parts) | (picks == parts + 16) | (picks == parts + 32)).astype(jnp.bfloat16)
    row_of = lax.broadcasted_iota(jnp.int32, (8, size), 0)
    for target, offset in enumerate(OFFSETS):
        ref, start = sources[offset]
        values = ref[:, start : start + size]
        if offset[0] != 0:
            values = jnp.where((row_of < 3) | inside(offset[0]), values, 0.0)
        high, middle, low = split(values)
        ones = jnp.ones_like(values)
        stacked = jnp.concatenate([high, high, middle, high, low, middle, ones, jnp.zeros_like(values)], 0)
        upright = stacked.T.astype(jnp.bfloat16)
        tall[target] = upright
        wide = lax.dot_general(upright, picks, (((1,), (0,)), ((), ())), preferred_element_type=jnp.float32)
        for part in range(4):
            column[target, part] = wide[:, part * LANES : (part + 1) * LANES]

    row_of = lax.broadcasted_iota(jnp.int32, (8, CHUNK), 0)
    base = STRETCH * (OBS_RADIUS * OBS_RADIUS + SOURCE_RADIUS * SOURCE_RADIUS)
    for at in range(obs.shape[0]):
        high, middle, low = split(jnp.where(row_of < 3, obs[at] * (-2.0 * STRETCH), 0.0))
        first, second, third = split(jnp.full((8, CHUNK), base, jnp.float32))
        constant = jnp.where(row_of == 0, first, jnp.where(row_of == 1, second, jnp.where(row_of == 2, third, 0.0)))
        stacked = jnp.concatenate([high, middle, high, low, high, middle, constant, jnp.zeros_like(high)], 0)
        flat[at] = stacked.astype(jnp.bfloat16)

    for tile in range(len(CROSS)):
        step = CROSS[tile]
        row = lat + step[0]
        first_row, last_row = row == 0, row == lat_tiles - 1
        own = (-step[0], -step[1])
        rest = [b for b in CROSS if b != own and b[0] == 0]
        ends = [b for b in CROSS if b != own and b[0] != 0]
        order = [OFFSETS.index((b[0] + step[0], b[1] + step[1])) for b in [own] + rest + ends]
        for at, target in enumerate(order):
            table[tile, at] = target
        if len(ends) == 2:
            table[tile, 3] = jnp.where(first_row, order[4], order[3])
            table[tile, 4] = jnp.where(first_row, order[3], order[4])
        members[tile] = 5 - first_row.astype(jnp.int32) - last_row.astype(jnp.int32)
        count = jnp.where(first_row | last_row, chunks, chunks // 2)
        counts[tile] = jnp.where(inside(step[0]), count, 0)

    total = jnp.int32(0)
    for full in (5, 4):
        for tile in (0, 3, 4, 1, 2):

            def note(chunk, at, tile=tile):
                items[0, at] = tile
                items[1, at] = tile * chunks + chunk
                return at + 1

            total = lax.fori_loop(0, jnp.where(members[tile] == full, counts[tile], 0), note, total)

    gram_ref[...] = jnp.zeros_like(gram_ref)
    held_odd[...] = jnp.zeros_like(held_odd)
    weighted_odd[...] = jnp.zeros_like(weighted_odd)
    right[...] = jnp.zeros_like(right)

    def separate(tile, chunk, at, apart):
        apart[at] = lax.dot_general(
            tall[table[tile, at]], flat[chunk], (((1,), (0,)), ((), ())), preferred_element_type=jnp.float32
        )

    def evaluate(tile, chunk, at, held, apart):
        target = table[tile, at]
        spare = (at != 0).astype(jnp.int32)
        point = [jnp.broadcast_to(obs[chunk, c : c + 1, :], (ROWS, CHUNK)) for c in range(3)]
        sums = [predicted[c] for c in range(3)]
        near = 1.5 * (OBS_RADIUS * OBS_RADIUS - SOURCE_RADIUS * SOURCE_RADIUS) * STRETCH
        for start in range(0, size, ROWS):
            span = slice(start, start + ROWS)
            wide = [jnp.concatenate([column[target, part, span, :]] * (CHUNK // LANES), axis=1) for part in range(4)]
            inverse = lax.rsqrt(apart[at, span, :])
            inverse_square = inverse * inverse
            cube = inverse_square * inverse
            along = near * inverse_square - 1.5
            for c in range(3):
                value = cube * (along * (point[c] - wide[c]) - wide[c])
                held[at, span, c * CHUNK : (c + 1) * CHUNK] = value.astype(jnp.bfloat16)
                kept[spare, c, span, :] = value
                part = value * wide[3]
                for sub in range(0, ROWS, 8):
                    sums[c] = sums[c] + part[sub : sub + 8]
        for c in range(3):
            predicted[c] = sums[c]

    def multiply(tile, at, held, weighted):
        target = table[tile, at]
        for half in (slice(0, size // 2), slice(size // 2, size)):
            gram_ref[target, half] += lax.dot_general(
                weighted[half], held[at], (((1,), (1,)), ((), ())), preferred_element_type=jnp.float32
            )

    def finish(chunk, weighted):
        present = obs[chunk, 6:7, :]
        scale, force = [], []
        for c in range(3):
            residual = obs[chunk, 3 + c : 4 + c, :] - jnp.sum(predicted[c], axis=0, keepdims=True)
            weight = present * HUBER_EDGE / jnp.maximum(jnp.abs(residual), HUBER_EDGE)
            scale.append(jnp.broadcast_to(weight, (ROWS, CHUNK)))
            force.append(jnp.broadcast_to(weight * residual, (ROWS, CHUNK)))
        for start in range(0, size, ROWS):
            span = slice(start, start + ROWS)
            pull = None
            for c in range(3):
                value = kept[0, c, span, :]
                weighted[span, c * CHUNK : (c + 1) * CHUNK] = (scale[c] * value).astype(jnp.bfloat16)
                part = force[c] * value
                pull = part if pull is None else pull + part
            for lane in range(0, CHUNK, LANES):
                right[span, :] += pull[:, lane : lane + LANES]

    def advance(item, held, weighted, apart, held_before, weighted_before, apart_later):
        tile, chunk = items[0, item], items[1, item]
        before = items[0, jnp.maximum(item - 1, 0)]
        after = jnp.minimum(item + 1, total - 1)
        later, later_chunk = items[0, after], items[1, after]
        predicted[...] = jnp.zeros_like(predicted)

        def block(at, carry):
            separate(later, later_chunk, at, apart_later)
            multiply(before, at, held_before, weighted_before)
            evaluate(tile, chunk, at, held, apart)
            return carry

        lax.fori_loop(0, members[before], block, 0)
        finish(chunk, weighted)

    def pair(at, carry):
        advance(2 * at, held_even, weighted_even, apart_even, held_odd, weighted_odd, apart_odd)
        advance(2 * at + 1, held_odd, weighted_odd, apart_odd, held_even, weighted_even, apart_even)
        return carry

    def open_item(at, carry):
        separate(items[0, 0], items[1, 0], at, apart_even)
        return carry

    lax.fori_loop(0, members[items[0, 0]], open_item, 0)
    lax.fori_loop(0, total // 2, pair, 0)
    last = items[0, total - 1]

    def drain(at, carry):
        multiply(last, at, held_odd, weighted_odd)
        return carry

    lax.fori_loop(0, members[last], drain, 0)

    for target, offset in enumerate(OFFSETS):
        if offset[0] != 0:

            @pl.when(jnp.logical_not(inside(offset[0])))
            def _():
                gram_ref[target] = jnp.zeros_like(gram_ref[target])

    rhs_ref[...] = jnp.sum(right[...].T, axis=0, keepdims=True)


def shards(obs_frac, obs_field, dipole_frac, dipole_moment, obs_count):
    lat_tiles = lax.axis_size("lat")
    lon_tiles = lax.axis_size("lon")
    lat_index = lax.axis_index("lat")
    lon_index = lax.axis_index("lon")
    size = dipole_frac.shape[3]
    slots = obs_frac.shape[3]
    source = place(dipole_frac[0, 0], lat_index, lon_index, lat_tiles, lon_tiles, SOURCE_RADIUS)
    points = place(obs_frac[0, 0], lat_index, lon_index, lat_tiles, lon_tiles, OBS_RADIUS)
    present = (jnp.arange(slots, dtype=jnp.int32) < obs_count[0, 0]).astype(jnp.float32)
    observed = jnp.concatenate([points, obs_field[0, 0], present[None], jnp.zeros((1, slots), jnp.float32)], 0)
    dipoles = jnp.concatenate([source, dipole_moment[0, 0][None], jnp.zeros((4, size), jnp.float32)], 0)
    package = jnp.concatenate([observed, dipoles], 1)
    north = cycled(package, "lat", 1)
    south = cycled(package, "lat", -1)
    west = cycled(package, "lon", 1)
    east = cycled(package, "lon", -1)
    far_north = cycled(jnp.concatenate([north[:, slots:], west[:, slots:], east[:, slots:]], 1), "lat", 1)
    far_south = cycled(jnp.concatenate([south[:, slots:], west[:, slots:], east[:, slots:]], 1), "lat", -1)
    far_west = cycled(west[:, slots:], "lon", 1)
    far_east = cycled(east[:, slots:], "lon", -1)
    chunks = slots // CHUNK
    gram, rhs = pl.pallas_call(
        functools.partial(row_kernel, lat_tiles=lat_tiles),
        out_shape=(
            jax.ShapeDtypeStruct((len(OFFSETS), size, size), jnp.float32),
            jax.ShapeDtypeStruct((1, size), jnp.float32),
        ),
        in_specs=[pl.BlockSpec(memory_space=pltpu.VMEM)] * 9,
        out_specs=(pl.BlockSpec(memory_space=pltpu.VMEM), pl.BlockSpec(memory_space=pltpu.VMEM)),
        scratch_shapes=[
            pltpu.VMEM((5 * chunks, 8, CHUNK), jnp.float32),
            pltpu.VMEM((len(OFFSETS), 4, size, LANES), jnp.float32),
            pltpu.VMEM((len(OFFSETS), size, DEPTH), jnp.bfloat16),
            pltpu.VMEM((5 * chunks, DEPTH, CHUNK), jnp.bfloat16),
            pltpu.VMEM((5, size, 3 * CHUNK), jnp.bfloat16),
            pltpu.VMEM((5, size, 3 * CHUNK), jnp.bfloat16),
            pltpu.VMEM((size, 3 * CHUNK), jnp.bfloat16),
            pltpu.VMEM((size, 3 * CHUNK), jnp.bfloat16),
            pltpu.VMEM((5, size, CHUNK), jnp.float32),
            pltpu.VMEM((5, size, CHUNK), jnp.float32),
            pltpu.VMEM((2, 3, size, CHUNK), jnp.float32),
            pltpu.VMEM((3, 8, CHUNK), jnp.float32),
            pltpu.VMEM((size, LANES), jnp.float32),
            pltpu.SMEM((5, 5), jnp.int32),
            pltpu.SMEM((2, 5 * chunks), jnp.int32),
            pltpu.SMEM((5,), jnp.int32),
            pltpu.SMEM((5,), jnp.int32),
        ],
        compiler_params=pltpu.CompilerParams(vmem_limit_bytes=60 * 1024 * 1024),
        name="row_blocks",
    )(package, north, south, west, east, far_north, far_south, far_west, far_east)
    return (gram[None, None], rhs[None])


def solution(mesh):
    in_specs = (
        P("lat", "lon", None, None),
        P("lat", "lon", None, None),
        P("lat", "lon", None, None),
        P("lat", "lon", None),
        P("lat", "lon"),
    )
    out_specs = (P("lat", "lon", None, None, None), P("lat", "lon", None))
    return jax.shard_map(shards, mesh=mesh, in_specs=in_specs, out_specs=out_specs, check_vma=False)
```

```python
import functools
import math

import jax
import jax.numpy as jnp
from jax import lax
from jax.experimental import pallas as pl
from jax.experimental.pallas import tpu as pltpu
from jax.sharding import PartitionSpec as P

CROSS = ((0, 0), (-1, 0), (1, 0), (0, -1), (0, 1))
OFFSETS = (
    (0, 0),
    (-1, 0),
    (1, 0),
    (0, -1),
    (0, 1),
    (-2, 0),
    (2, 0),
    (0, -2),
    (0, 2),
    (-1, -1),
    (-1, 1),
    (1, -1),
    (1, 1),
)
OBS_RADIUS = 1.06
SOURCE_RADIUS = 0.99
KERNEL_SCALE = 0.0001
HUBER_EDGE = 0.8
DEGREE = math.pi / 180.0
CHUNK = 512
ROWS = 16
LANES = 128
DEPTH = 64
STRETCH = KERNEL_SCALE ** (-2.0 / 3.0)


def cycled(value, axis, steps):
    count = lax.axis_size(axis)
    return lax.ppermute(value, axis, [(i, (i + steps) % count) for i in range(count)])


def place(fraction, lat_index, lon_index, lat_tiles, lon_tiles, radius):
    lat_span = 160.0 * DEGREE / lat_tiles
    latitude = -80.0 * DEGREE + (lat_index + fraction[0]) * lat_span
    longitude = (lon_index + fraction[1]) * (2.0 * math.pi / lon_tiles)
    return radius * jnp.stack(
        [
            jnp.cos(latitude) * jnp.cos(longitude),
            jnp.cos(latitude) * jnp.sin(longitude),
            jnp.sin(latitude),
        ]
    )


def split(values):
    high = values.astype(jnp.bfloat16).astype(jnp.float32)
    rest = values - high
    middle = rest.astype(jnp.bfloat16).astype(jnp.float32)
    return high, middle, rest - middle


def row_kernel(
    own_ref,
    north_ref,
    south_ref,
    west_ref,
    east_ref,
    far_north_ref,
    far_south_ref,
    far_west_ref,
    far_east_ref,
    gram_ref,
    rhs_ref,
    obs,
    column,
    tall,
    flat,
    held_even,
    held_odd,
    weighted_even,
    weighted_odd,
    apart_even,
    apart_odd,
    kept,
    predicted,
    right,
    table,
    items,
    members,
    counts,
    waits,
    gram,
    sent,
    *,
    lat_tiles,
):
    size = rhs_ref.shape[1]
    chunks = obs.shape[0] // len(CROSS)
    slots = chunks * CHUNK
    lat = lax.axis_index("lat")

    for tile, ref in enumerate((own_ref, north_ref, south_ref, west_ref, east_ref)):
        for chunk in range(chunks):
            obs[tile * chunks + chunk] = ref[:, chunk * CHUNK : (chunk + 1) * CHUNK]
    sources = {(0, 0): own_ref, (-1, 0): north_ref, (1, 0): south_ref, (0, -1): west_ref, (0, 1): east_ref}
    sources = {offset: (ref, slots) for offset, ref in sources.items()}
    for at, offset in enumerate(((-2, 0), (-1, -1), (-1, 1))):
        sources[offset] = (far_north_ref, at * size)
    for at, offset in enumerate(((2, 0), (1, -1), (1, 1))):
        sources[offset] = (far_south_ref, at * size)
    sources[(0, -2)] = (far_west_ref, 0)
    sources[(0, 2)] = (far_east_ref, 0)

    def inside(step):
        return (lat + step >= 0) & (lat + step < lat_tiles)

    picks = lax.broadcasted_iota(jnp.int32, (DEPTH, 4 * LANES), 0)
    parts = lax.broadcasted_iota(jnp.int32, (DEPTH, 4 * LANES), 1) // LANES
    picks = ((picks == parts) | (picks == parts + 16) | (picks == parts + 32)).astype(jnp.bfloat16)
    row_of = lax.broadcasted_iota(jnp.int32, (8, size), 0)
    for target, offset in enumerate(OFFSETS):
        ref, start = sources[offset]
        values = ref[:, start : start + size]
        if offset[0] != 0:
            values = jnp.where((row_of < 3) | inside(offset[0]), values, 0.0)
        high, middle, low = split(values)
        ones = jnp.ones_like(values)
        stacked = jnp.concatenate([high, high, middle, high, low, middle, ones, jnp.zeros_like(values)], 0)
        upright = stacked.T.astype(jnp.bfloat16)
        tall[target] = upright
        wide = lax.dot_general(upright, picks, (((1,), (0,)), ((), ())), preferred_element_type=jnp.float32)
        for part in range(4):
            column[target, part] = wide[:, part * LANES : (part + 1) * LANES]

    row_of = lax.broadcasted_iota(jnp.int32, (8, CHUNK), 0)
    base = STRETCH * (OBS_RADIUS * OBS_RADIUS + SOURCE_RADIUS * SOURCE_RADIUS)
    for at in range(obs.shape[0]):
        high, middle, low = split(jnp.where(row_of < 3, obs[at] * (-2.0 * STRETCH), 0.0))
        first, second, third = split(jnp.full((8, CHUNK), base, jnp.float32))
        constant = jnp.where(row_of == 0, first, jnp.where(row_of == 1, second, jnp.where(row_of == 2, third, 0.0)))
        stacked = jnp.concatenate([high, middle, high, low, high, middle, constant, jnp.zeros_like(high)], 0)
        flat[at] = stacked.astype(jnp.bfloat16)

    for tile in range(len(CROSS)):
        step = CROSS[tile]
        row = lat + step[0]
        first_row, last_row = row == 0, row == lat_tiles - 1
        own = (-step[0], -step[1])
        rest = [b for b in CROSS if b != own and b[0] == 0]
        ends = [b for b in CROSS if b != own and b[0] != 0]
        order = [OFFSETS.index((b[0] + step[0], b[1] + step[1])) for b in [own] + rest + ends]
        for at, target in enumerate(order):
            table[tile, at] = target
        if len(ends) == 2:
            table[tile, 3] = jnp.where(first_row, order[4], order[3])
            table[tile, 4] = jnp.where(first_row, order[3], order[4])
        members[tile] = 5 - first_row.astype(jnp.int32) - last_row.astype(jnp.int32)
        count = jnp.where(first_row | last_row, chunks, chunks // 2)
        counts[tile] = jnp.where(inside(step[0]), count, 0)

    total = jnp.int32(0)
    for full in (5, 4):
        for tile in (0, 3, 4, 1, 2):

            def note(chunk, at, tile=tile):
                items[0, at] = tile
                items[1, at] = tile * chunks + chunk
                return at + 1

            total = lax.fori_loop(0, jnp.where(members[tile] == full, counts[tile], 0), note, total)

    gram[...] = jnp.zeros_like(gram)
    held_odd[...] = jnp.zeros_like(held_odd)
    weighted_odd[...] = jnp.zeros_like(weighted_odd)
    right[...] = jnp.zeros_like(right)

    def separate(tile, chunk, at, apart):
        apart[at] = lax.dot_general(
            tall[table[tile, at]], flat[chunk], (((1,), (0,)), ((), ())), preferred_element_type=jnp.float32
        )

    def evaluate(tile, chunk, at, held, apart):
        target = table[tile, at]
        spare = (at != 0).astype(jnp.int32)
        point = [jnp.broadcast_to(obs[chunk, c : c + 1, :], (ROWS, CHUNK)) for c in range(3)]
        sums = [predicted[c] for c in range(3)]
        near = 1.5 * (OBS_RADIUS * OBS_RADIUS - SOURCE_RADIUS * SOURCE_RADIUS) * STRETCH
        for start in range(0, size, ROWS):
            span = slice(start, start + ROWS)
            wide = [jnp.concatenate([column[target, part, span, :]] * (CHUNK // LANES), axis=1) for part in range(4)]
            inverse = lax.rsqrt(apart[at, span, :])
            inverse_square = inverse * inverse
            cube = inverse_square * inverse
            along = near * inverse_square - 1.5
            for c in range(3):
                value = cube * (along * (point[c] - wide[c]) - wide[c])
                held[at, span, c * CHUNK : (c + 1) * CHUNK] = value.astype(jnp.bfloat16)
                kept[spare, c, span, :] = value
                part = value * wide[3]
                for sub in range(0, ROWS, 8):
                    sums[c] = sums[c] + part[sub : sub + 8]
        for c in range(3):
            predicted[c] = sums[c]

    def multiply(tile, at, held, weighted):
        target = table[tile, at]
        for half in (slice(0, size // 2), slice(size // 2, size)):
            gram[target, half] += lax.dot_general(
                held[at, half], weighted[...], (((1,), (0,)), ((), ())), preferred_element_type=jnp.float32
            )

    def flush(target):
        gram[target] = gram[target].T
        pltpu.make_async_copy(gram.at[target], gram_ref.at[target], sent.at[target]).start()

    def finish(chunk, weighted):
        present = obs[chunk, 6:7, :]
        scale, force = [], []
        for c in range(3):
            residual = obs[chunk, 3 + c : 4 + c, :] - jnp.sum(predicted[c], axis=0, keepdims=True)
            weight = present * HUBER_EDGE / jnp.maximum(jnp.abs(residual), HUBER_EDGE)
            scale.append(jnp.broadcast_to(weight, (ROWS, CHUNK)))
            force.append(jnp.broadcast_to(weight * residual, (ROWS, CHUNK)))
        for start in range(0, size, LANES):
            span = slice(start, start + LANES)
            for lane in range(0, CHUNK, LANES):
                over = slice(lane, lane + LANES)
                pull = right[span, :]
                for c in range(3):
                    value = kept[0, c, span, over]
                    scaled = (jnp.broadcast_to(scale[c][:1, over], (LANES, LANES)) * value).astype(jnp.bfloat16)
                    weighted[c * CHUNK + lane : c * CHUNK + lane + LANES, span] = scaled.T
                    pull = pull + jnp.broadcast_to(force[c][:1, over], (LANES, LANES)) * value
                right[span, :] = pull

    def advance(item, held, weighted, apart, held_before, weighted_before, apart_later):
        tile, chunk = items[0, item], items[1, item]
        before = items[0, jnp.maximum(item - 1, 0)]
        after = jnp.minimum(item + 1, total - 1)
        later, later_chunk = items[0, after], items[1, after]
        predicted[...] = jnp.zeros_like(predicted)

        def block(at, carry):
            separate(later, later_chunk, at, apart_later)
            multiply(before, at, held_before, weighted_before)
            evaluate(tile, chunk, at, held, apart)
            return carry

        lax.fori_loop(0, members[before], block, 0)
        finish(chunk, weighted)

    def pair(at, carry):
        advance(2 * at, held_even, weighted_even, apart_even, held_odd, weighted_odd, apart_odd)
        advance(2 * at + 1, held_odd, weighted_odd, apart_odd, held_even, weighted_even, apart_even)
        return carry

    def open_item(at, carry):
        separate(items[0, 0], items[1, 0], at, apart_even)
        return carry

    lax.fori_loop(0, members[items[0, 0]], open_item, 0)
    lax.fori_loop(0, total // 2, pair, 0)
    odd = total % 2 == 1
    last = items[0, total - 1]

    @pl.when(odd)
    def _():
        advance(total - 1, held_even, weighted_even, apart_even, held_odd, weighted_odd, apart_odd)

    for target in range(len(OFFSETS)):
        waits[target] = 0

    def mark(at, carry):
        waits[table[last, at]] = 1
        return carry

    lax.fori_loop(0, members[last], mark, 0)

    for target, offset in enumerate(OFFSETS):
        if offset[0] != 0:

            @pl.when(jnp.logical_not(inside(offset[0])))
            def _():
                gram[target] = jnp.zeros_like(gram[target])

    def early(target, carry):
        @pl.when(waits[target] == 0)
        def _():
            flush(target)

        return carry

    lax.fori_loop(0, len(OFFSETS), early, 0)

    def drain(held, weighted):
        def block(at, carry):
            multiply(last, at, held, weighted)
            flush(table[last, at])
            return carry

        lax.fori_loop(0, members[last], block, 0)

    @pl.when(odd)
    def _():
        drain(held_even, weighted_even)

    @pl.when(jnp.logical_not(odd))
    def _():
        drain(held_odd, weighted_odd)

    rhs_ref[...] = jnp.sum(right[...].T, axis=0, keepdims=True)

    def close(target, carry):
        pltpu.make_async_copy(gram.at[target], gram_ref.at[target], sent.at[target]).wait()
        return carry

    lax.fori_loop(0, len(OFFSETS), close, 0)


def shards(obs_frac, obs_field, dipole_frac, dipole_moment, obs_count):
    lat_tiles = lax.axis_size("lat")
    lon_tiles = lax.axis_size("lon")
    lat_index = lax.axis_index("lat")
    lon_index = lax.axis_index("lon")
    size = dipole_frac.shape[3]
    slots = obs_frac.shape[3]
    source = place(dipole_frac[0, 0], lat_index, lon_index, lat_tiles, lon_tiles, SOURCE_RADIUS)
    points = place(obs_frac[0, 0], lat_index, lon_index, lat_tiles, lon_tiles, OBS_RADIUS)
    present = (jnp.arange(slots, dtype=jnp.int32) < obs_count[0, 0]).astype(jnp.float32)
    observed = jnp.concatenate([points, obs_field[0, 0], present[None], jnp.zeros((1, slots), jnp.float32)], 0)
    dipoles = jnp.concatenate([source, dipole_moment[0, 0][None], jnp.zeros((4, size), jnp.float32)], 0)
    package = jnp.concatenate([observed, dipoles], 1)
    north = cycled(package, "lat", 1)
    south = cycled(package, "lat", -1)
    west = cycled(package, "lon", 1)
    east = cycled(package, "lon", -1)
    far_north = cycled(jnp.concatenate([north[:, slots:], west[:, slots:], east[:, slots:]], 1), "lat", 1)
    far_south = cycled(jnp.concatenate([south[:, slots:], west[:, slots:], east[:, slots:]], 1), "lat", -1)
    far_west = cycled(west[:, slots:], "lon", 1)
    far_east = cycled(east[:, slots:], "lon", -1)
    chunks = slots // CHUNK
    gram, rhs = pl.pallas_call(
        functools.partial(row_kernel, lat_tiles=lat_tiles),
        out_shape=(
            jax.ShapeDtypeStruct((len(OFFSETS), size, size), jnp.float32),
            jax.ShapeDtypeStruct((1, size), jnp.float32),
        ),
        in_specs=[pl.BlockSpec(memory_space=pltpu.VMEM)] * 9,
        out_specs=(pl.BlockSpec(memory_space=pl.ANY), pl.BlockSpec(memory_space=pltpu.VMEM)),
        scratch_shapes=[
            pltpu.VMEM((5 * chunks, 8, CHUNK), jnp.float32),
            pltpu.VMEM((len(OFFSETS), 4, size, LANES), jnp.float32),
            pltpu.VMEM((len(OFFSETS), size, DEPTH), jnp.bfloat16),
            pltpu.VMEM((5 * chunks, DEPTH, CHUNK), jnp.bfloat16),
            pltpu.VMEM((5, size, 3 * CHUNK), jnp.bfloat16),
            pltpu.VMEM((5, size, 3 * CHUNK), jnp.bfloat16),
            pltpu.VMEM((3 * CHUNK, size), jnp.bfloat16),
            pltpu.VMEM((3 * CHUNK, size), jnp.bfloat16),
            pltpu.VMEM((5, size, CHUNK), jnp.float32),
            pltpu.VMEM((5, size, CHUNK), jnp.float32),
            pltpu.VMEM((2, 3, size, CHUNK), jnp.float32),
            pltpu.VMEM((3, 8, CHUNK), jnp.float32),
            pltpu.VMEM((size, LANES), jnp.float32),
            pltpu.SMEM((5, 5), jnp.int32),
            pltpu.SMEM((2, 5 * chunks), jnp.int32),
            pltpu.SMEM((5,), jnp.int32),
            pltpu.SMEM((5,), jnp.int32),
            pltpu.SMEM((len(OFFSETS),), jnp.int32),
            pltpu.VMEM((len(OFFSETS), size, size), jnp.float32),
            pltpu.SemaphoreType.DMA((len(OFFSETS),)),
        ],
        compiler_params=pltpu.CompilerParams(vmem_limit_bytes=44 * 1024 * 1024),
        name="row_blocks",
    )(package, north, south, west, east, far_north, far_south, far_west, far_east)
    return (gram[None, None], rhs[None])


def solution(mesh):
    in_specs = (
        P("lat", "lon", None, None),
        P("lat", "lon", None, None),
        P("lat", "lon", None, None),
        P("lat", "lon", None),
        P("lat", "lon"),
    )
    out_specs = (P("lat", "lon", None, None, None), P("lat", "lon", None))
    return jax.shard_map(shards, mesh=mesh, in_specs=in_specs, out_specs=out_specs, check_vma=False)
```

```python
import functools
import math

import jax
import jax.numpy as jnp
from jax import lax
from jax.experimental import pallas as pl
from jax.experimental.pallas import tpu as pltpu
from jax.sharding import PartitionSpec as P

CROSS = ((0, 0), (-1, 0), (1, 0), (0, -1), (0, 1))
OFFSETS = (
    (0, 0),
    (-1, 0),
    (1, 0),
    (0, -1),
    (0, 1),
    (-2, 0),
    (2, 0),
    (0, -2),
    (0, 2),
    (-1, -1),
    (-1, 1),
    (1, -1),
    (1, 1),
)
OBS_RADIUS = 1.06
SOURCE_RADIUS = 0.99
KERNEL_SCALE = 0.0001
HUBER_EDGE = 0.8
DEGREE = math.pi / 180.0
CHUNK = 512
ROWS = 16
LANES = 128
DEPTH = 64
STRETCH = KERNEL_SCALE ** (-2.0 / 3.0)


def cycled(value, axis, steps):
    count = lax.axis_size(axis)
    return lax.ppermute(value, axis, [(i, (i + steps) % count) for i in range(count)])


def place(fraction, lat_index, lon_index, lat_tiles, lon_tiles, radius):
    lat_span = 160.0 * DEGREE / lat_tiles
    latitude = -80.0 * DEGREE + (lat_index + fraction[0]) * lat_span
    longitude = (lon_index + fraction[1]) * (2.0 * math.pi / lon_tiles)
    return radius * jnp.stack(
        [
            jnp.cos(latitude) * jnp.cos(longitude),
            jnp.cos(latitude) * jnp.sin(longitude),
            jnp.sin(latitude),
        ]
    )


def split(values):
    high = values.astype(jnp.bfloat16).astype(jnp.float32)
    rest = values - high
    middle = rest.astype(jnp.bfloat16).astype(jnp.float32)
    return high, middle, rest - middle


def row_kernel(
    own_ref,
    north_ref,
    south_ref,
    west_ref,
    east_ref,
    far_north_ref,
    far_south_ref,
    far_west_ref,
    far_east_ref,
    gram_ref,
    rhs_ref,
    obs,
    column,
    tall,
    flat,
    held_even,
    held_odd,
    weighted_even,
    weighted_odd,
    apart_even,
    apart_odd,
    kept,
    predicted,
    right,
    table,
    items,
    members,
    counts,
    waits,
    gram,
    sent,
    *,
    lat_tiles,
):
    size = rhs_ref.shape[1]
    chunks = obs.shape[0] // len(CROSS)
    slots = chunks * CHUNK
    lat = lax.axis_index("lat")

    for tile, ref in enumerate((own_ref, north_ref, south_ref, west_ref, east_ref)):
        for chunk in range(chunks):
            obs[tile * chunks + chunk] = ref[:, chunk * CHUNK : (chunk + 1) * CHUNK]
    sources = {(0, 0): own_ref, (-1, 0): north_ref, (1, 0): south_ref, (0, -1): west_ref, (0, 1): east_ref}
    sources = {offset: (ref, slots) for offset, ref in sources.items()}
    for at, offset in enumerate(((-2, 0), (-1, -1), (-1, 1))):
        sources[offset] = (far_north_ref, at * size)
    for at, offset in enumerate(((2, 0), (1, -1), (1, 1))):
        sources[offset] = (far_south_ref, at * size)
    sources[(0, -2)] = (far_west_ref, 0)
    sources[(0, 2)] = (far_east_ref, 0)

    def inside(step):
        return (lat + step >= 0) & (lat + step < lat_tiles)

    picks = lax.broadcasted_iota(jnp.int32, (DEPTH, 4 * LANES), 0)
    parts = lax.broadcasted_iota(jnp.int32, (DEPTH, 4 * LANES), 1) // LANES
    picks = ((picks == parts) | (picks == parts + 16) | (picks == parts + 32)).astype(jnp.bfloat16)
    row_of = lax.broadcasted_iota(jnp.int32, (8, size), 0)
    for target, offset in enumerate(OFFSETS):
        ref, start = sources[offset]
        values = ref[:, start : start + size]
        if offset[0] != 0:
            values = jnp.where((row_of < 3) | inside(offset[0]), values, 0.0)
        high, middle, low = split(values)
        ones = jnp.ones_like(values)
        stacked = jnp.concatenate([high, high, middle, high, low, middle, ones, jnp.zeros_like(values)], 0)
        upright = stacked.T.astype(jnp.bfloat16)
        tall[target] = upright
        wide = lax.dot_general(upright, picks, (((1,), (0,)), ((), ())), preferred_element_type=jnp.float32)
        for part in range(4):
            column[target, part] = wide[:, part * LANES : (part + 1) * LANES]

    row_of = lax.broadcasted_iota(jnp.int32, (8, CHUNK), 0)
    base = STRETCH * (OBS_RADIUS * OBS_RADIUS + SOURCE_RADIUS * SOURCE_RADIUS)
    for at in range(obs.shape[0]):
        high, middle, low = split(jnp.where(row_of < 3, obs[at] * (-2.0 * STRETCH), 0.0))
        first, second, third = split(jnp.full((8, CHUNK), base, jnp.float32))
        constant = jnp.where(row_of == 0, first, jnp.where(row_of == 1, second, jnp.where(row_of == 2, third, 0.0)))
        stacked = jnp.concatenate([high, middle, high, low, high, middle, constant, jnp.zeros_like(high)], 0)
        flat[at] = stacked.astype(jnp.bfloat16)

    for tile in range(len(CROSS)):
        step = CROSS[tile]
        row = lat + step[0]
        first_row, last_row = row == 0, row == lat_tiles - 1
        own = (-step[0], -step[1])
        rest = [b for b in CROSS if b != own and b[0] == 0]
        ends = [b for b in CROSS if b != own and b[0] != 0]
        order = [OFFSETS.index((b[0] + step[0], b[1] + step[1])) for b in [own] + rest + ends]
        for at, target in enumerate(order):
            table[tile, at] = target
        if len(ends) == 2:
            table[tile, 3] = jnp.where(first_row, order[4], order[3])
            table[tile, 4] = jnp.where(first_row, order[3], order[4])
        members[tile] = 5 - first_row.astype(jnp.int32) - last_row.astype(jnp.int32)
        count = jnp.where(first_row | last_row, chunks, chunks // 2)
        counts[tile] = jnp.where(inside(step[0]), count, 0)

    total = jnp.int32(0)
    for full in (5, 4):
        for tile in (0, 3, 4, 1, 2):

            def note(chunk, at, tile=tile):
                items[0, at] = tile
                items[1, at] = tile * chunks + chunk
                return at + 1

            total = lax.fori_loop(0, jnp.where(members[tile] == full, counts[tile], 0), note, total)

    gram[...] = jnp.zeros_like(gram)
    held_odd[...] = jnp.zeros_like(held_odd)
    weighted_odd[...] = jnp.zeros_like(weighted_odd)
    right[...] = jnp.zeros_like(right)

    def separate(tile, chunk, at, apart):
        apart[at] = lax.dot_general(
            tall[table[tile, at]], flat[chunk], (((1,), (0,)), ((), ())), preferred_element_type=jnp.float32
        )

    def evaluate(tile, chunk, at, held, apart):
        target = table[tile, at]
        spare = (at != 0).astype(jnp.int32)
        point = [jnp.broadcast_to(obs[chunk, c : c + 1, :], (ROWS, CHUNK)) for c in range(3)]
        sums = [predicted[c] for c in range(3)]
        near = 1.5 * (OBS_RADIUS * OBS_RADIUS - SOURCE_RADIUS * SOURCE_RADIUS) * STRETCH
        for start in range(0, size, ROWS):
            span = slice(start, start + ROWS)
            wide = [jnp.concatenate([column[target, part, span, :]] * (CHUNK // LANES), axis=1) for part in range(4)]
            inverse = lax.rsqrt(apart[at, span, :])
            inverse_square = inverse * inverse
            cube = inverse_square * inverse
            along = cube * (near * inverse_square - 1.5)
            across = along + cube
            for c in range(3):
                value = along * point[c] - across * wide[c]
                held[at, span, c * CHUNK : (c + 1) * CHUNK] = value.astype(jnp.bfloat16)
                kept[spare, c, span, :] = value
                part = value * wide[3]
                for sub in range(0, ROWS, 8):
                    sums[c] = sums[c] + part[sub : sub + 8]
        for c in range(3):
            predicted[c] = sums[c]

    def multiply(tile, at, held, weighted):
        target = table[tile, at]
        for half in (slice(0, size // 2), slice(size // 2, size)):
            gram[target, half] += lax.dot_general(
                held[at, half], weighted[...], (((1,), (0,)), ((), ())), preferred_element_type=jnp.float32
            )

    def flush(target):
        gram[target] = gram[target].T
        pltpu.make_async_copy(gram.at[target], gram_ref.at[target], sent.at[target]).start()

    def finish(chunk, weighted):
        present = obs[chunk, 6:7, :]
        scale, force = [], []
        for c in range(3):
            residual = obs[chunk, 3 + c : 4 + c, :] - jnp.sum(predicted[c], axis=0, keepdims=True)
            weight = present * HUBER_EDGE / jnp.maximum(jnp.abs(residual), HUBER_EDGE)
            scale.append(jnp.broadcast_to(weight, (ROWS, CHUNK)))
            force.append(jnp.broadcast_to(weight * residual, (ROWS, CHUNK)))
        for start in range(0, size, LANES):
            span = slice(start, start + LANES)
            for lane in range(0, CHUNK, LANES):
                over = slice(lane, lane + LANES)
                pull = right[span, :]
                for c in range(3):
                    value = kept[0, c, span, over]
                    scaled = (jnp.broadcast_to(scale[c][:1, over], (LANES, LANES)) * value).astype(jnp.bfloat16)
                    weighted[c * CHUNK + lane : c * CHUNK + lane + LANES, span] = scaled.T
                    pull = pull + jnp.broadcast_to(force[c][:1, over], (LANES, LANES)) * value
                right[span, :] = pull

    def advance(item, held, weighted, apart, held_before, weighted_before, apart_later):
        tile, chunk = items[0, item], items[1, item]
        before = items[0, jnp.maximum(item - 1, 0)]
        after = jnp.minimum(item + 1, total - 1)
        later, later_chunk = items[0, after], items[1, after]
        predicted[...] = jnp.zeros_like(predicted)

        def block(at, carry):
            separate(later, later_chunk, at, apart_later)
            multiply(before, at, held_before, weighted_before)
            evaluate(tile, chunk, at, held, apart)
            return carry

        lax.fori_loop(0, members[before], block, 0)
        finish(chunk, weighted)

    def pair(at, carry):
        advance(2 * at, held_even, weighted_even, apart_even, held_odd, weighted_odd, apart_odd)
        advance(2 * at + 1, held_odd, weighted_odd, apart_odd, held_even, weighted_even, apart_even)
        return carry

    def open_item(at, carry):
        separate(items[0, 0], items[1, 0], at, apart_even)
        return carry

    lax.fori_loop(0, members[items[0, 0]], open_item, 0)
    lax.fori_loop(0, total // 2, pair, 0)
    odd = total % 2 == 1
    last = items[0, total - 1]

    @pl.when(odd)
    def _():
        advance(total - 1, held_even, weighted_even, apart_even, held_odd, weighted_odd, apart_odd)

    for target in range(len(OFFSETS)):
        waits[target] = 0

    def mark(at, carry):
        waits[table[last, at]] = 1
        return carry

    lax.fori_loop(0, members[last], mark, 0)

    for target, offset in enumerate(OFFSETS):
        if offset[0] != 0:

            @pl.when(jnp.logical_not(inside(offset[0])))
            def _():
                gram[target] = jnp.zeros_like(gram[target])

    def early(target, carry):
        @pl.when(waits[target] == 0)
        def _():
            flush(target)

        return carry

    lax.fori_loop(0, len(OFFSETS), early, 0)

    def drain(held, weighted):
        def block(at, carry):
            multiply(last, at, held, weighted)
            flush(table[last, at])
            return carry

        lax.fori_loop(0, members[last], block, 0)

    @pl.when(odd)
    def _():
        drain(held_even, weighted_even)

    @pl.when(jnp.logical_not(odd))
    def _():
        drain(held_odd, weighted_odd)

    rhs_ref[...] = jnp.sum(right[...].T, axis=0, keepdims=True)

    def close(target, carry):
        pltpu.make_async_copy(gram.at[target], gram_ref.at[target], sent.at[target]).wait()
        return carry

    lax.fori_loop(0, len(OFFSETS), close, 0)


def shards(obs_frac, obs_field, dipole_frac, dipole_moment, obs_count):
    lat_tiles = lax.axis_size("lat")
    lon_tiles = lax.axis_size("lon")
    lat_index = lax.axis_index("lat")
    lon_index = lax.axis_index("lon")
    size = dipole_frac.shape[3]
    slots = obs_frac.shape[3]
    source = place(dipole_frac[0, 0], lat_index, lon_index, lat_tiles, lon_tiles, SOURCE_RADIUS)
    points = place(obs_frac[0, 0], lat_index, lon_index, lat_tiles, lon_tiles, OBS_RADIUS)
    present = (jnp.arange(slots, dtype=jnp.int32) < obs_count[0, 0]).astype(jnp.float32)
    observed = jnp.concatenate([points, obs_field[0, 0], present[None], jnp.zeros((1, slots), jnp.float32)], 0)
    dipoles = jnp.concatenate([source, dipole_moment[0, 0][None], jnp.zeros((4, size), jnp.float32)], 0)
    package = jnp.concatenate([observed, dipoles], 1)
    north = cycled(package, "lat", 1)
    south = cycled(package, "lat", -1)
    west = cycled(package, "lon", 1)
    east = cycled(package, "lon", -1)
    far_north = cycled(jnp.concatenate([north[:, slots:], west[:, slots:], east[:, slots:]], 1), "lat", 1)
    far_south = cycled(jnp.concatenate([south[:, slots:], west[:, slots:], east[:, slots:]], 1), "lat", -1)
    far_west = cycled(dipoles, "lon", 2)
    far_east = far_west if lon_tiles == 4 else cycled(dipoles, "lon", -2)
    chunks = slots // CHUNK
    gram, rhs = pl.pallas_call(
        functools.partial(row_kernel, lat_tiles=lat_tiles),
        out_shape=(
            jax.ShapeDtypeStruct((len(OFFSETS), size, size), jnp.float32),
            jax.ShapeDtypeStruct((1, size), jnp.float32),
        ),
        in_specs=[pl.BlockSpec(memory_space=pltpu.VMEM)] * 9,
        out_specs=(pl.BlockSpec(memory_space=pl.ANY), pl.BlockSpec(memory_space=pltpu.VMEM)),
        scratch_shapes=[
            pltpu.VMEM((5 * chunks, 8, CHUNK), jnp.float32),
            pltpu.VMEM((len(OFFSETS), 4, size, LANES), jnp.float32),
            pltpu.VMEM((len(OFFSETS), size, DEPTH), jnp.bfloat16),
            pltpu.VMEM((5 * chunks, DEPTH, CHUNK), jnp.bfloat16),
            pltpu.VMEM((5, size, 3 * CHUNK), jnp.bfloat16),
            pltpu.VMEM((5, size, 3 * CHUNK), jnp.bfloat16),
            pltpu.VMEM((3 * CHUNK, size), jnp.bfloat16),
            pltpu.VMEM((3 * CHUNK, size), jnp.bfloat16),
            pltpu.VMEM((5, size, CHUNK), jnp.float32),
            pltpu.VMEM((5, size, CHUNK), jnp.float32),
            pltpu.VMEM((2, 3, size, CHUNK), jnp.float32),
            pltpu.VMEM((3, 8, CHUNK), jnp.float32),
            pltpu.VMEM((size, LANES), jnp.float32),
            pltpu.SMEM((5, 5), jnp.int32),
            pltpu.SMEM((2, 5 * chunks), jnp.int32),
            pltpu.SMEM((5,), jnp.int32),
            pltpu.SMEM((5,), jnp.int32),
            pltpu.SMEM((len(OFFSETS),), jnp.int32),
            pltpu.VMEM((len(OFFSETS), size, size), jnp.float32),
            pltpu.SemaphoreType.DMA((len(OFFSETS),)),
        ],
        compiler_params=pltpu.CompilerParams(vmem_limit_bytes=44 * 1024 * 1024),
        name="row_blocks",
    )(package, north, south, west, east, far_north, far_south, far_west, far_east)
    return (gram[None, None], rhs[None])


def solution(mesh):
    in_specs = (
        P("lat", "lon", None, None),
        P("lat", "lon", None, None),
        P("lat", "lon", None, None),
        P("lat", "lon", None),
        P("lat", "lon"),
    )
    out_specs = (P("lat", "lon", None, None, None), P("lat", "lon", None))
    return jax.shard_map(shards, mesh=mesh, in_specs=in_specs, out_specs=out_specs, check_vma=False)
```

```python
import functools
import math

import jax
import jax.numpy as jnp
from jax import lax
from jax.experimental import pallas as pl
from jax.experimental.pallas import tpu as pltpu
from jax.sharding import PartitionSpec as P

CROSS = ((0, 0), (-1, 0), (1, 0), (0, -1), (0, 1))
OFFSETS = (
    (0, 0),
    (-1, 0),
    (1, 0),
    (0, -1),
    (0, 1),
    (-2, 0),
    (2, 0),
    (0, -2),
    (0, 2),
    (-1, -1),
    (-1, 1),
    (1, -1),
    (1, 1),
)
OBS_RADIUS = 1.06
SOURCE_RADIUS = 0.99
KERNEL_SCALE = 0.0001
HUBER_EDGE = 0.8
DEGREE = math.pi / 180.0
CHUNK = 512
ROWS = 16
LANES = 128
DEPTH = 64
STRETCH = KERNEL_SCALE ** (-2.0 / 3.0)


def cycled(value, axis, steps):
    count = lax.axis_size(axis)
    return lax.ppermute(value, axis, [(i, (i + steps) % count) for i in range(count)])


def pack_kernel(
    obs_frac_ref, obs_field_ref, dipole_frac_ref, moment_ref, obs_count, package, dipoles,
    obs_frac, obs_field, dipole_frac, moment, landed, *, lat_tiles, lon_tiles,
):
    loads = [
        pltpu.make_async_copy(source, target, landed.at[at])
        for at, (source, target) in enumerate(
            ((obs_frac_ref, obs_frac), (obs_field_ref, obs_field), (dipole_frac_ref, dipole_frac), (moment_ref, moment))
        )
    ]
    for load in loads:
        load.start()
    for load in loads:
        load.wait()
    lat_index = lax.axis_index("lat").astype(jnp.float32)
    lon_index = lax.axis_index("lon").astype(jnp.float32)
    lat_span = 160.0 * DEGREE / lat_tiles
    lon_span = 2.0 * math.pi / lon_tiles

    def place(fraction, radius):
        row = lax.broadcasted_iota(jnp.int32, fraction.shape, 0)
        angle = jnp.where(row == 0, -80.0 * DEGREE + (lat_index + fraction) * lat_span, (lon_index + fraction) * lon_span)
        cosine, sine = jnp.cos(angle), jnp.sin(angle)
        return [
            radius * (cosine[0:1] * cosine[1:2]),
            radius * (cosine[0:1] * sine[1:2]),
            radius * sine[0:1],
        ]

    slots, size = obs_frac.shape[1], dipole_frac.shape[1]
    for row, value in enumerate(place(obs_frac[...], OBS_RADIUS)):
        package[row : row + 1, :slots] = value
    package[3:6, :slots] = obs_field[...]
    index = lax.broadcasted_iota(jnp.int32, (1, slots), 1)
    package[6:7, :slots] = (index < obs_count[0, 0]).astype(jnp.float32)
    package[7:8, :slots] = jnp.zeros((1, slots), jnp.float32)
    rows = place(dipole_frac[...], SOURCE_RADIUS) + [moment[...], jnp.zeros((4, size), jnp.float32)]
    filled = jnp.concatenate(rows, 0)
    package[:, slots:] = filled
    dipoles[...] = filled


def split(values):
    high = values.astype(jnp.bfloat16).astype(jnp.float32)
    rest = values - high
    middle = rest.astype(jnp.bfloat16).astype(jnp.float32)
    return high, middle, rest - middle


def row_kernel(
    own_ref,
    north_ref,
    south_ref,
    west_ref,
    east_ref,
    far_north_ref,
    far_south_ref,
    far_west_ref,
    far_east_ref,
    gram_ref,
    rhs_ref,
    obs,
    column,
    tall,
    flat,
    held_even,
    held_odd,
    weighted_even,
    weighted_odd,
    apart_even,
    apart_odd,
    kept,
    predicted,
    right,
    table,
    items,
    members,
    counts,
    waits,
    gram,
    sent,
    *,
    lat_tiles,
):
    size = rhs_ref.shape[1]
    chunks = obs.shape[0] // len(CROSS)
    slots = chunks * CHUNK
    lat = lax.axis_index("lat")

    for tile, ref in enumerate((own_ref, north_ref, south_ref, west_ref, east_ref)):
        for chunk in range(chunks):
            obs[tile * chunks + chunk] = ref[:, chunk * CHUNK : (chunk + 1) * CHUNK]
    sources = {(0, 0): own_ref, (-1, 0): north_ref, (1, 0): south_ref, (0, -1): west_ref, (0, 1): east_ref}
    sources = {offset: (ref, slots) for offset, ref in sources.items()}
    for at, offset in enumerate(((-2, 0), (-1, -1), (-1, 1))):
        sources[offset] = (far_north_ref, at * size)
    for at, offset in enumerate(((2, 0), (1, -1), (1, 1))):
        sources[offset] = (far_south_ref, at * size)
    sources[(0, -2)] = (far_west_ref, 0)
    sources[(0, 2)] = (far_east_ref, 0)

    def inside(step):
        return (lat + step >= 0) & (lat + step < lat_tiles)

    picks = lax.broadcasted_iota(jnp.int32, (DEPTH, 4 * LANES), 0)
    parts = lax.broadcasted_iota(jnp.int32, (DEPTH, 4 * LANES), 1) // LANES
    picks = ((picks == parts) | (picks == parts + 16) | (picks == parts + 32)).astype(jnp.bfloat16)
    row_of = lax.broadcasted_iota(jnp.int32, (8, size), 0)
    right[...] = jnp.zeros_like(right)
    for target, offset in enumerate(OFFSETS):
        ref, start = sources[offset]
        values = ref[:, start : start + size]
        if offset[0] != 0:
            values = jnp.where((row_of < 3) | inside(offset[0]), values, 0.0)
        high, middle, low = split(values)
        ones = jnp.ones_like(values)
        stacked = jnp.concatenate([high, high, middle, high, low, middle, ones, jnp.zeros_like(values)], 0)
        upright = stacked.T.astype(jnp.bfloat16)
        gram[target] = jnp.zeros((size, size), jnp.float32)
        tall[target] = upright
        wide = lax.dot_general(upright, picks, (((1,), (0,)), ((), ())), preferred_element_type=jnp.float32)
        for part in range(4):
            column[target, part] = wide[:, part * LANES : (part + 1) * LANES]

    row_of = lax.broadcasted_iota(jnp.int32, (8, CHUNK), 0)
    base = STRETCH * (OBS_RADIUS * OBS_RADIUS + SOURCE_RADIUS * SOURCE_RADIUS)
    for at in range(obs.shape[0]):
        high, middle, low = split(jnp.where(row_of < 3, obs[at] * (-2.0 * STRETCH), 0.0))
        first, second, third = split(jnp.full((8, CHUNK), base, jnp.float32))
        constant = jnp.where(row_of == 0, first, jnp.where(row_of == 1, second, jnp.where(row_of == 2, third, 0.0)))
        stacked = jnp.concatenate([high, middle, high, low, high, middle, constant, jnp.zeros_like(high)], 0)
        flat[at] = stacked.astype(jnp.bfloat16)

    for tile in range(len(CROSS)):
        step = CROSS[tile]
        row = lat + step[0]
        first_row, last_row = row == 0, row == lat_tiles - 1
        own = (-step[0], -step[1])
        rest = [b for b in CROSS if b != own and b[0] == 0]
        ends = [b for b in CROSS if b != own and b[0] != 0]
        order = [OFFSETS.index((b[0] + step[0], b[1] + step[1])) for b in [own] + rest + ends]
        for at, target in enumerate(order):
            table[tile, at] = target
        if len(ends) == 2:
            table[tile, 3] = jnp.where(first_row, order[4], order[3])
            table[tile, 4] = jnp.where(first_row, order[3], order[4])
        members[tile] = 5 - first_row.astype(jnp.int32) - last_row.astype(jnp.int32)
        count = jnp.where(first_row | last_row, chunks, chunks // 2)
        counts[tile] = jnp.where(inside(step[0]), count, 0)

    total = jnp.int32(0)
    for full in (5, 4):
        for tile in (0, 3, 4, 1, 2):

            def note(chunk, at, tile=tile):
                items[0, at] = tile
                items[1, at] = tile * chunks + chunk
                return at + 1

            total = lax.fori_loop(0, jnp.where(members[tile] == full, counts[tile], 0), note, total)


    def separate(tile, chunk, at, apart):
        apart[at] = lax.dot_general(
            tall[table[tile, at]], flat[chunk], (((1,), (0,)), ((), ())), preferred_element_type=jnp.float32
        )

    def evaluate(tile, chunk, at, held, apart):
        target = table[tile, at]
        spare = (at != 0).astype(jnp.int32)
        point = [jnp.broadcast_to(obs[chunk, c : c + 1, :], (ROWS, CHUNK)) for c in range(3)]
        sums = [predicted[c] for c in range(3)]
        near = 1.5 * (OBS_RADIUS * OBS_RADIUS - SOURCE_RADIUS * SOURCE_RADIUS) * STRETCH
        for start in range(0, size, ROWS):
            span = slice(start, start + ROWS)
            wide = [jnp.concatenate([column[target, part, span, :]] * (CHUNK // LANES), axis=1) for part in range(4)]
            inverse = lax.rsqrt(apart[at, span, :])
            inverse_square = inverse * inverse
            cube = inverse_square * inverse
            along = cube * (near * inverse_square - 1.5)
            across = along + cube
            for c in range(3):
                value = along * point[c] - across * wide[c]
                held[at, span, c * CHUNK : (c + 1) * CHUNK] = value.astype(jnp.bfloat16)
                kept[spare, c, span, :] = value
                part = value * wide[3]
                for sub in range(0, ROWS, 8):
                    sums[c] = sums[c] + part[sub : sub + 8]
        for c in range(3):
            predicted[c] = sums[c]

    def multiply(target, at, held, weighted):
        for half in (slice(0, size // 2), slice(size // 2, size)):
            gram[target, half] += lax.dot_general(
                held[at, half], weighted[...], (((1,), (0,)), ((), ())), preferred_element_type=jnp.float32
            )

    def flush(target):
        gram[target] = gram[target].T
        pltpu.make_async_copy(gram.at[target], gram_ref.at[target], sent.at[target]).start()

    def finish(chunk, weighted):
        present = obs[chunk, 6:7, :]
        scale, force = [], []
        for c in range(3):
            residual = obs[chunk, 3 + c : 4 + c, :] - jnp.sum(predicted[c], axis=0, keepdims=True)
            weight = present * HUBER_EDGE / jnp.maximum(jnp.abs(residual), HUBER_EDGE)
            scale.append(jnp.broadcast_to(weight, (ROWS, CHUNK)))
            force.append(jnp.broadcast_to(weight * residual, (ROWS, CHUNK)))
        for start in range(0, size, LANES):
            span = slice(start, start + LANES)
            for lane in range(0, CHUNK, LANES):
                over = slice(lane, lane + LANES)
                pull = right[span, :]
                for c in range(3):
                    value = kept[0, c, span, over]
                    scaled = (jnp.broadcast_to(scale[c][:1, over], (LANES, LANES)) * value).astype(jnp.bfloat16)
                    weighted[c * CHUNK + lane : c * CHUNK + lane + LANES, span] = scaled.T
                    pull = pull + jnp.broadcast_to(force[c][:1, over], (LANES, LANES)) * value
                right[span, :] = pull

    last = items[0, total - 1]
    twice = items[0, jnp.maximum(total - 2, 0)] == last

    def clear(target, carry):
        waits[target] = 0
        return carry

    lax.fori_loop(0, len(OFFSETS), clear, 0)

    def mark(at, carry):
        waits[table[last, at]] = 1
        return carry

    lax.fori_loop(0, members[last], mark, 0)

    def early(target, carry):
        @pl.when(waits[target] == 0)
        def _():
            flush(target)

        return carry

    def advance(item, held, weighted, apart, held_before, weighted_before, apart_later):
        tile, chunk = items[0, item], items[1, item]
        before = items[0, jnp.maximum(item - 1, 0)]
        after = jnp.minimum(item + 1, total - 1)
        later, later_chunk = items[0, after], items[1, after]
        predicted[...] = jnp.zeros_like(predicted)

        @pl.when((item == total - 1) & twice)
        def _():
            lax.fori_loop(0, len(OFFSETS), early, 0)

        def block(at, carry):
            separate(later, later_chunk, at, apart_later)
            target = jnp.where(item == 0, len(OFFSETS), table[before, at])
            multiply(target, at, held_before, weighted_before)
            evaluate(tile, chunk, at, held, apart)
            return carry

        lax.fori_loop(0, members[before], block, 0)
        finish(chunk, weighted)

    def pair(at, carry):
        advance(2 * at, held_even, weighted_even, apart_even, held_odd, weighted_odd, apart_odd)
        advance(2 * at + 1, held_odd, weighted_odd, apart_odd, held_even, weighted_even, apart_even)
        return carry

    def open_item(at, carry):
        separate(items[0, 0], items[1, 0], at, apart_even)
        return carry

    lax.fori_loop(0, members[items[0, 0]], open_item, 0)
    lax.fori_loop(0, total // 2, pair, 0)
    odd = total % 2 == 1

    @pl.when(odd)
    def _():
        advance(total - 1, held_even, weighted_even, apart_even, held_odd, weighted_odd, apart_odd)

    @pl.when(jnp.logical_not(twice))
    def _():
        lax.fori_loop(0, len(OFFSETS), early, 0)

    def drain(held, weighted):
        def block(at, carry):
            multiply(table[last, at], at, held, weighted)
            flush(table[last, at])
            return carry

        lax.fori_loop(0, members[last], block, 0)

    @pl.when(odd)
    def _():
        drain(held_even, weighted_even)

    @pl.when(jnp.logical_not(odd))
    def _():
        drain(held_odd, weighted_odd)

    rhs_ref[...] = jnp.sum(right[...].T, axis=0, keepdims=True)

    def close(target, carry):
        pltpu.make_async_copy(gram.at[target], gram_ref.at[target], sent.at[target]).wait()
        return carry

    lax.fori_loop(0, len(OFFSETS), close, 0)


def shards(obs_frac, obs_field, dipole_frac, dipole_moment, obs_count):
    lat_tiles = lax.axis_size("lat")
    lon_tiles = lax.axis_size("lon")
    size = dipole_frac.shape[3]
    slots = obs_frac.shape[3]
    package, dipoles = pl.pallas_call(
        functools.partial(pack_kernel, lat_tiles=lat_tiles, lon_tiles=lon_tiles),
        out_shape=(
            jax.ShapeDtypeStruct((8, slots + size), jnp.float32),
            jax.ShapeDtypeStruct((8, size), jnp.float32),
        ),
        in_specs=[pl.BlockSpec(memory_space=pltpu.HBM)] * 4 + [pl.BlockSpec(memory_space=pltpu.SMEM)],
        out_specs=(pl.BlockSpec(memory_space=pltpu.VMEM), pl.BlockSpec(memory_space=pltpu.VMEM)),
        scratch_shapes=[
            pltpu.VMEM((2, slots), jnp.float32),
            pltpu.VMEM((3, slots), jnp.float32),
            pltpu.VMEM((2, size), jnp.float32),
            pltpu.VMEM((1, size), jnp.float32),
            pltpu.SemaphoreType.DMA((4,)),
        ],
        compiler_params=pltpu.CompilerParams(vmem_limit_bytes=4 * 1024 * 1024),
        name="pack_tile",
    )(obs_frac[0, 0], obs_field[0, 0], dipole_frac[0, 0], dipole_moment[0], obs_count)
    north = cycled(package, "lat", 1)
    south = cycled(package, "lat", -1)
    far_west = cycled(dipoles, "lon", 2)
    far_east = far_west if lon_tiles == 4 else cycled(dipoles, "lon", -2)
    west = cycled(package, "lon", 1)
    east = cycled(package, "lon", -1)
    north, south, far_west, far_east, west, east = lax.optimization_barrier((north, south, far_west, far_east, west, east))
    far_north = cycled(jnp.concatenate([north[:, slots:], west[:, slots:], east[:, slots:]], 1), "lat", 1)
    far_south = cycled(jnp.concatenate([south[:, slots:], west[:, slots:], east[:, slots:]], 1), "lat", -1)
    chunks = slots // CHUNK
    gram, rhs = pl.pallas_call(
        functools.partial(row_kernel, lat_tiles=lat_tiles),
        out_shape=(
            jax.ShapeDtypeStruct((len(OFFSETS), size, size), jnp.float32),
            jax.ShapeDtypeStruct((1, size), jnp.float32),
        ),
        in_specs=[pl.BlockSpec(memory_space=pltpu.VMEM)] * 9,
        out_specs=(pl.BlockSpec(memory_space=pl.ANY), pl.BlockSpec(memory_space=pltpu.VMEM)),
        scratch_shapes=[
            pltpu.VMEM((5 * chunks, 8, CHUNK), jnp.float32),
            pltpu.VMEM((len(OFFSETS), 4, size, LANES), jnp.float32),
            pltpu.VMEM((len(OFFSETS), size, DEPTH), jnp.bfloat16),
            pltpu.VMEM((5 * chunks, DEPTH, CHUNK), jnp.bfloat16),
            pltpu.VMEM((5, size, 3 * CHUNK), jnp.bfloat16),
            pltpu.VMEM((5, size, 3 * CHUNK), jnp.bfloat16),
            pltpu.VMEM((3 * CHUNK, size), jnp.bfloat16),
            pltpu.VMEM((3 * CHUNK, size), jnp.bfloat16),
            pltpu.VMEM((5, size, CHUNK), jnp.float32),
            pltpu.VMEM((5, size, CHUNK), jnp.float32),
            pltpu.VMEM((2, 3, size, CHUNK), jnp.float32),
            pltpu.VMEM((3, 8, CHUNK), jnp.float32),
            pltpu.VMEM((size, LANES), jnp.float32),
            pltpu.SMEM((5, 5), jnp.int32),
            pltpu.SMEM((2, 5 * chunks), jnp.int32),
            pltpu.SMEM((5,), jnp.int32),
            pltpu.SMEM((5,), jnp.int32),
            pltpu.SMEM((len(OFFSETS),), jnp.int32),
            pltpu.VMEM((len(OFFSETS) + 1, size, size), jnp.float32),
            pltpu.SemaphoreType.DMA((len(OFFSETS),)),
        ],
        compiler_params=pltpu.CompilerParams(vmem_limit_bytes=44 * 1024 * 1024),
        name="row_blocks",
    )(package, north, south, west, east, far_north, far_south, far_west, far_east)
    return (gram[None, None], rhs[None])


def solution(mesh):
    in_specs = (
        P("lat", "lon", None, None),
        P("lat", "lon", None, None),
        P("lat", "lon", None, None),
        P("lat", "lon", None),
        P("lat", "lon"),
    )
    out_specs = (P("lat", "lon", None, None, None), P("lat", "lon", None))
    return jax.shard_map(shards, mesh=mesh, in_specs=in_specs, out_specs=out_specs, check_vma=False)
```

```python
import functools
import math

import jax
import jax.numpy as jnp
from jax import lax
from jax.experimental import pallas as pl
from jax.experimental.pallas import tpu as pltpu
from jax.sharding import PartitionSpec as P

CROSS = ((0, 0), (-1, 0), (1, 0), (0, -1), (0, 1))
OFFSETS = (
    (0, 0),
    (-1, 0),
    (1, 0),
    (0, -1),
    (0, 1),
    (-2, 0),
    (2, 0),
    (0, -2),
    (0, 2),
    (-1, -1),
    (-1, 1),
    (1, -1),
    (1, 1),
)
OBS_RADIUS = 1.06
SOURCE_RADIUS = 0.99
KERNEL_SCALE = 0.0001
HUBER_EDGE = 0.8
DEGREE = math.pi / 180.0
CHUNK = 512
ROWS = 16
LANES = 128
DEPTH = 64
STRETCH = KERNEL_SCALE ** (-2.0 / 3.0)


def cycled(value, axis, steps):
    count = lax.axis_size(axis)
    return lax.ppermute(value, axis, [(i, (i + steps) % count) for i in range(count)])


def pack_kernel(
    obs_frac_ref, obs_field_ref, dipole_frac_ref, moment_ref, obs_count, package, dipoles,
    obs_frac, obs_field, dipole_frac, moment, landed, *, lat_tiles, lon_tiles,
):
    loads = [
        pltpu.make_async_copy(source, target, landed.at[at])
        for at, (source, target) in enumerate(
            ((obs_frac_ref, obs_frac), (obs_field_ref, obs_field), (dipole_frac_ref, dipole_frac), (moment_ref, moment))
        )
    ]
    for load in loads:
        load.start()
    for load in loads:
        load.wait()
    lat_index = lax.axis_index("lat").astype(jnp.float32)
    lon_index = lax.axis_index("lon").astype(jnp.float32)
    lat_span = 160.0 * DEGREE / lat_tiles
    lon_span = 2.0 * math.pi / lon_tiles

    def place(fraction, radius):
        row = lax.broadcasted_iota(jnp.int32, fraction.shape, 0)
        angle = jnp.where(row == 0, -80.0 * DEGREE + (lat_index + fraction) * lat_span, (lon_index + fraction) * lon_span)
        cosine, sine = jnp.cos(angle), jnp.sin(angle)
        return [
            radius * (cosine[0:1] * cosine[1:2]),
            radius * (cosine[0:1] * sine[1:2]),
            radius * sine[0:1],
        ]

    slots, size = obs_frac.shape[1], dipole_frac.shape[1]
    for row, value in enumerate(place(obs_frac[...], OBS_RADIUS)):
        package[row : row + 1, :slots] = value
    package[3:6, :slots] = obs_field[...]
    index = lax.broadcasted_iota(jnp.int32, (1, slots), 1)
    package[6:7, :slots] = (index < obs_count[0, 0]).astype(jnp.float32)
    package[7:8, :slots] = jnp.zeros((1, slots), jnp.float32)
    rows = place(dipole_frac[...], SOURCE_RADIUS) + [moment[...], jnp.zeros((4, size), jnp.float32)]
    filled = jnp.concatenate(rows, 0)
    package[:, slots:] = filled
    dipoles[...] = filled


def split(values):
    high = values.astype(jnp.bfloat16).astype(jnp.float32)
    rest = values - high
    middle = rest.astype(jnp.bfloat16).astype(jnp.float32)
    return high, middle, rest - middle


def row_kernel(*refs, lat_tiles, opening):
    refs = list(refs)
    own_ref, north_ref, south_ref, west_ref, east_ref = refs[:5]
    if opening:
        gram, right = refs[5:7]
        rest = refs[7:]
        tiles, targets = (0,), range(len(CROSS))
    else:
        far_north_ref, far_south_ref, far_west_ref, far_east_ref, gram_in, right_in, gram_ref, rhs_ref = refs[5:13]
        rest = refs[13:]
        tiles, targets = (3, 4, 1, 2), range(len(OFFSETS))
    (
        obs,
        column,
        tall,
        flat,
        held_even,
        held_odd,
        weighted_even,
        weighted_odd,
        apart_even,
        apart_odd,
        kept,
        predicted,
        table,
        items,
        members,
        counts,
    ) = rest[:16]
    if not opening:
        right, waits, gram, sent = rest[16:]
    size = right.shape[0]
    chunks = obs.shape[0] // len(CROSS)
    slots = chunks * CHUNK
    lat = lax.axis_index("lat")

    arrived = (own_ref, north_ref, south_ref, west_ref, east_ref)
    for tile in tiles:
        for chunk in range(chunks):
            obs[tile * chunks + chunk] = arrived[tile][:, chunk * CHUNK : (chunk + 1) * CHUNK]
    sources = {offset: (ref, slots) for offset, ref in zip(CROSS, arrived)}
    if not opening:
        for at, offset in enumerate(((-2, 0), (-1, -1), (-1, 1))):
            sources[offset] = (far_north_ref, at * size)
        for at, offset in enumerate(((2, 0), (1, -1), (1, 1))):
            sources[offset] = (far_south_ref, at * size)
        sources[(0, -2)] = (far_west_ref, 0)
        sources[(0, 2)] = (far_east_ref, 0)

    def inside(step):
        return (lat + step >= 0) & (lat + step < lat_tiles)

    picks = lax.broadcasted_iota(jnp.int32, (DEPTH, 4 * LANES), 0)
    parts = lax.broadcasted_iota(jnp.int32, (DEPTH, 4 * LANES), 1) // LANES
    picks = ((picks == parts) | (picks == parts + 16) | (picks == parts + 32)).astype(jnp.bfloat16)
    row_of = lax.broadcasted_iota(jnp.int32, (8, size), 0)
    right[...] = jnp.zeros_like(right) if opening else right_in[...]
    for target in targets:
        offset = OFFSETS[target]
        ref, start = sources[offset]
        values = ref[:, start : start + size]
        if offset[0] != 0:
            values = jnp.where((row_of < 3) | inside(offset[0]), values, 0.0)
        high, middle, low = split(values)
        ones = jnp.ones_like(values)
        stacked = jnp.concatenate([high, high, middle, high, low, middle, ones, jnp.zeros_like(values)], 0)
        upright = stacked.T.astype(jnp.bfloat16)
        fresh = opening or target >= len(CROSS)
        gram[target] = jnp.zeros((size, size), jnp.float32) if fresh else gram_in[target]
        tall[target] = upright
        wide = lax.dot_general(upright, picks, (((1,), (0,)), ((), ())), preferred_element_type=jnp.float32)
        for part in range(4):
            column[target, part] = wide[:, part * LANES : (part + 1) * LANES]

    row_of = lax.broadcasted_iota(jnp.int32, (8, CHUNK), 0)
    base = STRETCH * (OBS_RADIUS * OBS_RADIUS + SOURCE_RADIUS * SOURCE_RADIUS)
    for at in [tile * chunks + chunk for tile in tiles for chunk in range(chunks)]:
        high, middle, low = split(jnp.where(row_of < 3, obs[at] * (-2.0 * STRETCH), 0.0))
        first, second, third = split(jnp.full((8, CHUNK), base, jnp.float32))
        constant = jnp.where(row_of == 0, first, jnp.where(row_of == 1, second, jnp.where(row_of == 2, third, 0.0)))
        stacked = jnp.concatenate([high, middle, high, low, high, middle, constant, jnp.zeros_like(high)], 0)
        flat[at] = stacked.astype(jnp.bfloat16)

    for tile in tiles:
        step = CROSS[tile]
        row = lat + step[0]
        first_row, last_row = row == 0, row == lat_tiles - 1
        own = (-step[0], -step[1])
        rest = [b for b in CROSS if b != own and b[0] == 0]
        ends = [b for b in CROSS if b != own and b[0] != 0]
        order = [OFFSETS.index((b[0] + step[0], b[1] + step[1])) for b in [own] + rest + ends]
        for at, target in enumerate(order):
            table[tile, at] = target
        if len(ends) == 2:
            table[tile, 3] = jnp.where(first_row, order[4], order[3])
            table[tile, 4] = jnp.where(first_row, order[3], order[4])
        members[tile] = 5 - first_row.astype(jnp.int32) - last_row.astype(jnp.int32)
        count = jnp.where(first_row | last_row, chunks, chunks // 2)
        counts[tile] = jnp.where(inside(step[0]), count, 0)

    total = jnp.int32(0)
    for full in (5, 4):
        for tile in tiles:

            def note(chunk, at, tile=tile):
                items[0, at] = tile
                items[1, at] = tile * chunks + chunk
                return at + 1

            total = lax.fori_loop(0, jnp.where(members[tile] == full, counts[tile], 0), note, total)


    def separate(tile, chunk, at, apart):
        apart[at] = lax.dot_general(
            tall[table[tile, at]], flat[chunk], (((1,), (0,)), ((), ())), preferred_element_type=jnp.float32
        )

    def evaluate(tile, chunk, at, held, apart):
        target = table[tile, at]
        spare = (at != 0).astype(jnp.int32)
        point = [jnp.broadcast_to(obs[chunk, c : c + 1, :], (ROWS, CHUNK)) for c in range(3)]
        sums = [predicted[c] for c in range(3)]
        near = 1.5 * (OBS_RADIUS * OBS_RADIUS - SOURCE_RADIUS * SOURCE_RADIUS) * STRETCH
        for start in range(0, size, ROWS):
            span = slice(start, start + ROWS)
            wide = [jnp.concatenate([column[target, part, span, :]] * (CHUNK // LANES), axis=1) for part in range(4)]
            inverse = lax.rsqrt(apart[at, span, :])
            inverse_square = inverse * inverse
            cube = inverse_square * inverse
            along = cube * (near * inverse_square - 1.5)
            across = along + cube
            for c in range(3):
                value = along * point[c] - across * wide[c]
                held[at, span, c * CHUNK : (c + 1) * CHUNK] = value.astype(jnp.bfloat16)
                kept[spare, c, span, :] = value
                part = value * wide[3]
                for sub in range(0, ROWS, 8):
                    sums[c] = sums[c] + part[sub : sub + 8]
        for c in range(3):
            predicted[c] = sums[c]

    def multiply(target, at, held, weighted):
        for half in (slice(0, size // 2), slice(size // 2, size)):
            gram[target, half] += lax.dot_general(
                held[at, half], weighted[...], (((1,), (0,)), ((), ())), preferred_element_type=jnp.float32
            )

    def flush(target):
        gram[target] = gram[target].T
        pltpu.make_async_copy(gram.at[target], gram_ref.at[target], sent.at[target]).start()

    def finish(chunk, weighted):
        present = obs[chunk, 6:7, :]
        scale, force = [], []
        for c in range(3):
            residual = obs[chunk, 3 + c : 4 + c, :] - jnp.sum(predicted[c], axis=0, keepdims=True)
            weight = present * HUBER_EDGE / jnp.maximum(jnp.abs(residual), HUBER_EDGE)
            scale.append(jnp.broadcast_to(weight, (ROWS, CHUNK)))
            force.append(jnp.broadcast_to(weight * residual, (ROWS, CHUNK)))
        for start in range(0, size, LANES):
            span = slice(start, start + LANES)
            for lane in range(0, CHUNK, LANES):
                over = slice(lane, lane + LANES)
                pull = right[span, :]
                for c in range(3):
                    value = kept[0, c, span, over]
                    scaled = (jnp.broadcast_to(scale[c][:1, over], (LANES, LANES)) * value).astype(jnp.bfloat16)
                    weighted[c * CHUNK + lane : c * CHUNK + lane + LANES, span] = scaled.T
                    pull = pull + jnp.broadcast_to(force[c][:1, over], (LANES, LANES)) * value
                right[span, :] = pull

    last = items[0, total - 1]
    twice = items[0, jnp.maximum(total - 2, 0)] == last

    if not opening:

        def clear(target, carry):
            waits[target] = 0
            return carry

        lax.fori_loop(0, len(OFFSETS), clear, 0)

        def mark(at, carry):
            waits[table[last, at]] = 1
            return carry

        lax.fori_loop(0, members[last], mark, 0)

    def early(target, carry):
        @pl.when(waits[target] == 0)
        def _():
            flush(target)

        return carry

    def advance(item, held, weighted, apart, held_before, weighted_before, apart_later):
        tile, chunk = items[0, item], items[1, item]
        before = items[0, jnp.maximum(item - 1, 0)]
        after = jnp.minimum(item + 1, total - 1)
        later, later_chunk = items[0, after], items[1, after]
        predicted[...] = jnp.zeros_like(predicted)

        if not opening:

            @pl.when((item == total - 1) & twice)
            def _():
                lax.fori_loop(0, len(OFFSETS), early, 0)

        def block(at, carry):
            separate(later, later_chunk, at, apart_later)
            target = jnp.where(item == 0, len(targets), table[before, at])
            multiply(target, at, held_before, weighted_before)
            evaluate(tile, chunk, at, held, apart)
            return carry

        lax.fori_loop(0, members[before], block, 0)
        finish(chunk, weighted)

    def pair(at, carry):
        advance(2 * at, held_even, weighted_even, apart_even, held_odd, weighted_odd, apart_odd)
        advance(2 * at + 1, held_odd, weighted_odd, apart_odd, held_even, weighted_even, apart_even)
        return carry

    def open_item(at, carry):
        separate(items[0, 0], items[1, 0], at, apart_even)
        return carry

    lax.fori_loop(0, members[items[0, 0]], open_item, 0)
    lax.fori_loop(0, total // 2, pair, 0)
    odd = total % 2 == 1

    @pl.when(odd)
    def _():
        advance(total - 1, held_even, weighted_even, apart_even, held_odd, weighted_odd, apart_odd)

    if not opening:

        @pl.when(jnp.logical_not(twice))
        def _():
            lax.fori_loop(0, len(OFFSETS), early, 0)

    def drain(held, weighted):
        def block(at, carry):
            multiply(table[last, at], at, held, weighted)
            if not opening:
                flush(table[last, at])
            return carry

        lax.fori_loop(0, members[last], block, 0)

    @pl.when(odd)
    def _():
        drain(held_even, weighted_even)

    @pl.when(jnp.logical_not(odd))
    def _():
        drain(held_odd, weighted_odd)

    if not opening:
        rhs_ref[...] = jnp.sum(right[...].T, axis=0, keepdims=True)

        def close(target, carry):
            pltpu.make_async_copy(gram.at[target], gram_ref.at[target], sent.at[target]).wait()
            return carry

        lax.fori_loop(0, len(OFFSETS), close, 0)


def shards(obs_frac, obs_field, dipole_frac, dipole_moment, obs_count):
    lat_tiles = lax.axis_size("lat")
    lon_tiles = lax.axis_size("lon")
    size = dipole_frac.shape[3]
    slots = obs_frac.shape[3]
    package, dipoles = pl.pallas_call(
        functools.partial(pack_kernel, lat_tiles=lat_tiles, lon_tiles=lon_tiles),
        out_shape=(
            jax.ShapeDtypeStruct((8, slots + size), jnp.float32),
            jax.ShapeDtypeStruct((8, size), jnp.float32),
        ),
        in_specs=[pl.BlockSpec(memory_space=pltpu.HBM)] * 4 + [pl.BlockSpec(memory_space=pltpu.SMEM)],
        out_specs=(pl.BlockSpec(memory_space=pltpu.VMEM), pl.BlockSpec(memory_space=pltpu.VMEM)),
        scratch_shapes=[
            pltpu.VMEM((2, slots), jnp.float32),
            pltpu.VMEM((3, slots), jnp.float32),
            pltpu.VMEM((2, size), jnp.float32),
            pltpu.VMEM((1, size), jnp.float32),
            pltpu.SemaphoreType.DMA((4,)),
        ],
        compiler_params=pltpu.CompilerParams(vmem_limit_bytes=4 * 1024 * 1024),
        name="pack_tile",
    )(obs_frac[0, 0], obs_field[0, 0], dipole_frac[0, 0], dipole_moment[0], obs_count)
    north = cycled(package, "lat", 1)
    south = cycled(package, "lat", -1)
    far_west = cycled(dipoles, "lon", 2)
    far_east = far_west if lon_tiles == 4 else cycled(dipoles, "lon", -2)
    west = cycled(package, "lon", 1)
    east = cycled(package, "lon", -1)
    north, south, far_west, far_east, west, east = lax.optimization_barrier((north, south, far_west, far_east, west, east))
    far_north = cycled(jnp.concatenate([north[:, slots:], west[:, slots:], east[:, slots:]], 1), "lat", 1)
    far_south = cycled(jnp.concatenate([south[:, slots:], west[:, slots:], east[:, slots:]], 1), "lat", -1)
    chunks = slots // CHUNK
    vmem = pl.BlockSpec(memory_space=pltpu.VMEM)

    def working(targets):
        return [
            pltpu.VMEM((5 * chunks, 8, CHUNK), jnp.float32),
            pltpu.VMEM((targets, 4, size, LANES), jnp.float32),
            pltpu.VMEM((targets, size, DEPTH), jnp.bfloat16),
            pltpu.VMEM((5 * chunks, DEPTH, CHUNK), jnp.bfloat16),
            pltpu.VMEM((5, size, 3 * CHUNK), jnp.bfloat16),
            pltpu.VMEM((5, size, 3 * CHUNK), jnp.bfloat16),
            pltpu.VMEM((3 * CHUNK, size), jnp.bfloat16),
            pltpu.VMEM((3 * CHUNK, size), jnp.bfloat16),
            pltpu.VMEM((5, size, CHUNK), jnp.float32),
            pltpu.VMEM((5, size, CHUNK), jnp.float32),
            pltpu.VMEM((2, 3, size, CHUNK), jnp.float32),
            pltpu.VMEM((3, 8, CHUNK), jnp.float32),
            pltpu.SMEM((5, 5), jnp.int32),
            pltpu.SMEM((2, 5 * chunks), jnp.int32),
            pltpu.SMEM((5,), jnp.int32),
            pltpu.SMEM((5,), jnp.int32),
        ]

    products = 2 * 3 * slots * size * size
    own_gram, own_right = pl.pallas_call(
        functools.partial(row_kernel, lat_tiles=lat_tiles, opening=True),
        out_shape=(
            jax.ShapeDtypeStruct((len(CROSS) + 1, size, size), jnp.float32),
            jax.ShapeDtypeStruct((size, LANES), jnp.float32),
        ),
        in_specs=[vmem] * 5,
        out_specs=(vmem, vmem),
        scratch_shapes=working(len(CROSS)),
        compiler_params=pltpu.CompilerParams(vmem_limit_bytes=26 * 1024 * 1024),
        cost_estimate=pl.CostEstimate(flops=5 * products, bytes_accessed=8 * size * size * 4, transcendentals=0),
        name="own_rows",
    )(package, north, south, west, east)
    gram, rhs = pl.pallas_call(
        functools.partial(row_kernel, lat_tiles=lat_tiles, opening=False),
        out_shape=(
            jax.ShapeDtypeStruct((len(OFFSETS), size, size), jnp.float32),
            jax.ShapeDtypeStruct((1, size), jnp.float32),
        ),
        in_specs=[vmem] * 11,
        out_specs=(pl.BlockSpec(memory_space=pl.ANY), vmem),
        scratch_shapes=working(len(OFFSETS))
        + [
            pltpu.VMEM((size, LANES), jnp.float32),
            pltpu.SMEM((len(OFFSETS),), jnp.int32),
            pltpu.VMEM((len(OFFSETS) + 1, size, size), jnp.float32),
            pltpu.SemaphoreType.DMA((len(OFFSETS),)),
        ],
        compiler_params=pltpu.CompilerParams(vmem_limit_bytes=44 * 1024 * 1024),
        cost_estimate=pl.CostEstimate(flops=20 * products, bytes_accessed=16 * size * size * 4, transcendentals=0),
        name="row_blocks",
    )(package, north, south, west, east, far_north, far_south, far_west, far_east, own_gram, own_right)
    return (gram[None, None], rhs[None])


def solution(mesh):
    in_specs = (
        P("lat", "lon", None, None),
        P("lat", "lon", None, None),
        P("lat", "lon", None, None),
        P("lat", "lon", None),
        P("lat", "lon"),
    )
    out_specs = (P("lat", "lon", None, None, None), P("lat", "lon", None))
    return jax.shard_map(shards, mesh=mesh, in_specs=in_specs, out_specs=out_specs, check_vma=False)
```

```python
import functools
import math

import jax
import jax.numpy as jnp
from jax import lax
from jax.experimental import pallas as pl
from jax.experimental.pallas import tpu as pltpu
from jax.sharding import PartitionSpec as P

CROSS = ((0, 0), (-1, 0), (1, 0), (0, -1), (0, 1))
OFFSETS = (
    (0, 0),
    (-1, 0),
    (1, 0),
    (0, -1),
    (0, 1),
    (-2, 0),
    (2, 0),
    (0, -2),
    (0, 2),
    (-1, -1),
    (-1, 1),
    (1, -1),
    (1, 1),
)
OBS_RADIUS = 1.06
SOURCE_RADIUS = 0.99
KERNEL_SCALE = 0.0001
HUBER_EDGE = 0.8
DEGREE = math.pi / 180.0
CHUNK = 512
ROWS = 16
LANES = 128
DEPTH = 64
STRETCH = KERNEL_SCALE ** (-2.0 / 3.0)


def cycled(value, axis, steps):
    count = lax.axis_size(axis)
    return lax.ppermute(value, axis, [(i, (i + steps) % count) for i in range(count)])


def pack_kernel(raw, obs_count, package, dipoles, *, lat_tiles, lon_tiles):
    size = dipoles.shape[1]
    slots = raw.shape[1] - size
    obs_frac, obs_field = raw[0:2, :slots], raw[2:5, :slots]
    dipole_frac, moment = raw[0:2, slots:], raw[2:3, slots:]
    lat_index = lax.axis_index("lat").astype(jnp.float32)
    lon_index = lax.axis_index("lon").astype(jnp.float32)
    lat_span = 160.0 * DEGREE / lat_tiles
    lon_span = 2.0 * math.pi / lon_tiles

    def place(fraction, radius):
        row = lax.broadcasted_iota(jnp.int32, fraction.shape, 0)
        angle = jnp.where(row == 0, -80.0 * DEGREE + (lat_index + fraction) * lat_span, (lon_index + fraction) * lon_span)
        cosine, sine = jnp.cos(angle), jnp.sin(angle)
        return [
            radius * (cosine[0:1] * cosine[1:2]),
            radius * (cosine[0:1] * sine[1:2]),
            radius * sine[0:1],
        ]

    for row, value in enumerate(place(obs_frac, OBS_RADIUS)):
        package[row : row + 1, :slots] = value
    package[3:6, :slots] = obs_field
    index = lax.broadcasted_iota(jnp.int32, (1, slots), 1)
    package[6:7, :slots] = (index < obs_count[0, 0]).astype(jnp.float32)
    package[7:8, :slots] = jnp.zeros((1, slots), jnp.float32)
    rows = place(dipole_frac, SOURCE_RADIUS) + [moment, jnp.zeros((4, size), jnp.float32)]
    filled = jnp.concatenate(rows, 0)
    package[:, slots:] = filled
    dipoles[...] = filled


def split(values):
    high = values.astype(jnp.bfloat16).astype(jnp.float32)
    rest = values - high
    middle = rest.astype(jnp.bfloat16).astype(jnp.float32)
    return high, middle, rest - middle


def row_kernel(*refs, lat_tiles, opening):
    refs = list(refs)
    own_ref, north_ref, south_ref, west_ref, east_ref = refs[:5]
    if opening:
        gram, right = refs[5:7]
        rest = refs[7:]
        tiles, targets = (0,), range(len(CROSS))
    else:
        far_north_ref, far_south_ref, far_west_ref, far_east_ref, gram_in, right_in, gram_ref, rhs_ref = refs[5:13]
        rest = refs[13:]
        tiles, targets = (3, 4, 1, 2), range(len(OFFSETS))
    (
        obs,
        column,
        tall,
        flat,
        held_even,
        held_odd,
        weighted_even,
        weighted_odd,
        apart_even,
        apart_odd,
        kept,
        predicted,
        table,
        items,
        members,
        counts,
    ) = rest[:16]
    if not opening:
        right, waits, gram, sent = rest[16:]
    size = right.shape[0]
    chunks = obs.shape[0] // len(CROSS)
    slots = chunks * CHUNK
    lat = lax.axis_index("lat")

    arrived = (own_ref, north_ref, south_ref, west_ref, east_ref)
    for tile in tiles:
        for chunk in range(chunks):
            obs[tile * chunks + chunk] = arrived[tile][:, chunk * CHUNK : (chunk + 1) * CHUNK]
    sources = {offset: (ref, slots) for offset, ref in zip(CROSS, arrived)}
    if not opening:
        for at, offset in enumerate(((-2, 0), (-1, -1), (-1, 1))):
            sources[offset] = (far_north_ref, at * size)
        for at, offset in enumerate(((2, 0), (1, -1), (1, 1))):
            sources[offset] = (far_south_ref, at * size)
        sources[(0, -2)] = (far_west_ref, 0)
        sources[(0, 2)] = (far_east_ref, 0)

    def inside(step):
        return (lat + step >= 0) & (lat + step < lat_tiles)

    picks = lax.broadcasted_iota(jnp.int32, (DEPTH, 4 * LANES), 0)
    parts = lax.broadcasted_iota(jnp.int32, (DEPTH, 4 * LANES), 1) // LANES
    picks = ((picks == parts) | (picks == parts + 16) | (picks == parts + 32)).astype(jnp.bfloat16)
    row_of = lax.broadcasted_iota(jnp.int32, (8, size), 0)
    right[...] = jnp.zeros_like(right) if opening else right_in[...]
    for target in targets:
        offset = OFFSETS[target]
        ref, start = sources[offset]
        values = ref[:, start : start + size]
        if offset[0] != 0:
            values = jnp.where((row_of < 3) | inside(offset[0]), values, 0.0)
        high, middle, low = split(values)
        ones = jnp.ones_like(values)
        stacked = jnp.concatenate([high, high, middle, high, low, middle, ones, jnp.zeros_like(values)], 0)
        upright = stacked.T.astype(jnp.bfloat16)
        fresh = opening or target >= len(CROSS)
        gram[target] = jnp.zeros((size, size), jnp.float32) if fresh else gram_in[target]
        tall[target] = upright
        wide = lax.dot_general(upright, picks, (((1,), (0,)), ((), ())), preferred_element_type=jnp.float32)
        for part in range(4):
            column[target, part] = wide[:, part * LANES : (part + 1) * LANES]

    row_of = lax.broadcasted_iota(jnp.int32, (8, CHUNK), 0)
    base = STRETCH * (OBS_RADIUS * OBS_RADIUS + SOURCE_RADIUS * SOURCE_RADIUS)
    for at in [tile * chunks + chunk for tile in tiles for chunk in range(chunks)]:
        high, middle, low = split(jnp.where(row_of < 3, obs[at] * (-2.0 * STRETCH), 0.0))
        first, second, third = split(jnp.full((8, CHUNK), base, jnp.float32))
        constant = jnp.where(row_of == 0, first, jnp.where(row_of == 1, second, jnp.where(row_of == 2, third, 0.0)))
        stacked = jnp.concatenate([high, middle, high, low, high, middle, constant, jnp.zeros_like(high)], 0)
        flat[at] = stacked.astype(jnp.bfloat16)

    for tile in tiles:
        step = CROSS[tile]
        row = lat + step[0]
        first_row, last_row = row == 0, row == lat_tiles - 1
        own = (-step[0], -step[1])
        rest = [b for b in CROSS if b != own and b[0] == 0]
        ends = [b for b in CROSS if b != own and b[0] != 0]
        order = [OFFSETS.index((b[0] + step[0], b[1] + step[1])) for b in [own] + rest + ends]
        for at, target in enumerate(order):
            table[tile, at] = target
        if len(ends) == 2:
            table[tile, 3] = jnp.where(first_row, order[4], order[3])
            table[tile, 4] = jnp.where(first_row, order[3], order[4])
        members[tile] = 5 - first_row.astype(jnp.int32) - last_row.astype(jnp.int32)
        count = jnp.where(first_row | last_row, chunks, chunks // 2)
        counts[tile] = jnp.where(inside(step[0]), count, 0)

    total = jnp.int32(0)
    for full in (5, 4):
        for tile in tiles:

            def note(chunk, at, tile=tile):
                items[0, at] = tile
                items[1, at] = tile * chunks + chunk
                return at + 1

            total = lax.fori_loop(0, jnp.where(members[tile] == full, counts[tile], 0), note, total)


    def separate(tile, chunk, at, apart):
        apart[at] = lax.dot_general(
            tall[table[tile, at]], flat[chunk], (((1,), (0,)), ((), ())), preferred_element_type=jnp.float32
        )

    def evaluate(tile, chunk, at, held, apart):
        target = table[tile, at]
        spare = (at != 0).astype(jnp.int32)
        point = [jnp.broadcast_to(obs[chunk, c : c + 1, :], (ROWS, CHUNK)) for c in range(3)]
        sums = [predicted[c] for c in range(3)]
        near = 1.5 * (OBS_RADIUS * OBS_RADIUS - SOURCE_RADIUS * SOURCE_RADIUS) * STRETCH
        for start in range(0, size, ROWS):
            span = slice(start, start + ROWS)
            wide = [jnp.concatenate([column[target, part, span, :]] * (CHUNK // LANES), axis=1) for part in range(4)]
            inverse = lax.rsqrt(apart[at, span, :])
            inverse_square = inverse * inverse
            cube = inverse_square * inverse
            along = cube * (near * inverse_square - 1.5)
            across = along + cube
            for c in range(3):
                value = along * point[c] - across * wide[c]
                held[at, span, c * CHUNK : (c + 1) * CHUNK] = value.astype(jnp.bfloat16)
                kept[spare, c, span, :] = value
                part = value * wide[3]
                for sub in range(0, ROWS, 8):
                    sums[c] = sums[c] + part[sub : sub + 8]
        for c in range(3):
            predicted[c] = sums[c]

    def multiply(target, at, held, weighted):
        for half in (slice(0, size // 2), slice(size // 2, size)):
            gram[target, half] += lax.dot_general(
                held[at, half], weighted[...], (((1,), (0,)), ((), ())), preferred_element_type=jnp.float32
            )

    def flush(target):
        gram[target] = gram[target].T
        pltpu.make_async_copy(gram.at[target], gram_ref.at[target], sent.at[target]).start()

    def finish(chunk, weighted):
        present = obs[chunk, 6:7, :]
        scale, force = [], []
        for c in range(3):
            residual = obs[chunk, 3 + c : 4 + c, :] - jnp.sum(predicted[c], axis=0, keepdims=True)
            weight = present * HUBER_EDGE / jnp.maximum(jnp.abs(residual), HUBER_EDGE)
            scale.append(jnp.broadcast_to(weight, (ROWS, CHUNK)))
            force.append(jnp.broadcast_to(weight * residual, (ROWS, CHUNK)))
        for start in range(0, size, LANES):
            span = slice(start, start + LANES)
            for lane in range(0, CHUNK, LANES):
                over = slice(lane, lane + LANES)
                pull = right[span, :]
                for c in range(3):
                    value = kept[0, c, span, over]
                    scaled = (jnp.concatenate([scale[c][:, over]] * (LANES // ROWS), axis=0) * value).astype(jnp.bfloat16)
                    weighted[c * CHUNK + lane : c * CHUNK + lane + LANES, span] = scaled.T
                    pull = pull + jnp.concatenate([force[c][:, over]] * (LANES // ROWS), axis=0) * value
                right[span, :] = pull

    last = items[0, total - 1]
    twice = items[0, jnp.maximum(total - 2, 0)] == last

    if not opening:

        def clear(target, carry):
            waits[target] = 0
            return carry

        lax.fori_loop(0, len(OFFSETS), clear, 0)

        def mark(at, carry):
            waits[table[last, at]] = 1
            return carry

        lax.fori_loop(0, members[last], mark, 0)

    def early(target, carry):
        @pl.when(waits[target] == 0)
        def _():
            flush(target)

        return carry

    def advance(item, held, weighted, apart, held_before, weighted_before, apart_later):
        tile, chunk = items[0, item], items[1, item]
        before = items[0, jnp.maximum(item - 1, 0)]
        after = jnp.minimum(item + 1, total - 1)
        later, later_chunk = items[0, after], items[1, after]
        predicted[...] = jnp.zeros_like(predicted)

        if not opening:

            @pl.when((item == total - 1) & twice)
            def _():
                lax.fori_loop(0, len(OFFSETS), early, 0)

        def block(at, carry):
            separate(later, later_chunk, at, apart_later)
            target = jnp.where(item == 0, len(targets), table[before, at])
            multiply(target, at, held_before, weighted_before)
            evaluate(tile, chunk, at, held, apart)
            return carry

        lax.fori_loop(0, members[before], block, 0)
        finish(chunk, weighted)

    def pair(at, carry):
        advance(2 * at, held_even, weighted_even, apart_even, held_odd, weighted_odd, apart_odd)
        advance(2 * at + 1, held_odd, weighted_odd, apart_odd, held_even, weighted_even, apart_even)
        return carry

    def open_item(at, carry):
        separate(items[0, 0], items[1, 0], at, apart_even)
        return carry

    lax.fori_loop(0, members[items[0, 0]], open_item, 0)
    lax.fori_loop(0, total // 2, pair, 0)
    odd = total % 2 == 1

    @pl.when(odd)
    def _():
        advance(total - 1, held_even, weighted_even, apart_even, held_odd, weighted_odd, apart_odd)

    if not opening:

        @pl.when(jnp.logical_not(twice))
        def _():
            lax.fori_loop(0, len(OFFSETS), early, 0)

    def drain(held, weighted):
        def block(at, carry):
            multiply(table[last, at], at, held, weighted)
            if not opening:
                flush(table[last, at])
            return carry

        lax.fori_loop(0, members[last], block, 0)

    @pl.when(odd)
    def _():
        drain(held_even, weighted_even)

    @pl.when(jnp.logical_not(odd))
    def _():
        drain(held_odd, weighted_odd)

    if not opening:
        rhs_ref[...] = jnp.sum(right[...].T, axis=0, keepdims=True)

        def close(target, carry):
            pltpu.make_async_copy(gram.at[target], gram_ref.at[target], sent.at[target]).wait()
            return carry

        lax.fori_loop(0, len(OFFSETS), close, 0)


def shards(obs_frac, obs_field, dipole_frac, dipole_moment, obs_count):
    lat_tiles = lax.axis_size("lat")
    lon_tiles = lax.axis_size("lon")
    size = dipole_frac.shape[3]
    slots = obs_frac.shape[3]
    observed = jnp.concatenate([obs_frac[0, 0], obs_field[0, 0], jnp.zeros((3, slots), jnp.float32)], 0)
    drawn = jnp.concatenate([dipole_frac[0, 0], dipole_moment[0], jnp.zeros((5, size), jnp.float32)], 0)
    raw = jnp.concatenate([observed, drawn], 1)
    package, dipoles = pl.pallas_call(
        functools.partial(pack_kernel, lat_tiles=lat_tiles, lon_tiles=lon_tiles),
        out_shape=(
            jax.ShapeDtypeStruct((8, slots + size), jnp.float32),
            jax.ShapeDtypeStruct((8, size), jnp.float32),
        ),
        in_specs=[pl.BlockSpec(memory_space=pltpu.VMEM), pl.BlockSpec(memory_space=pltpu.SMEM)],
        out_specs=(pl.BlockSpec(memory_space=pltpu.VMEM), pl.BlockSpec(memory_space=pltpu.VMEM)),
        compiler_params=pltpu.CompilerParams(vmem_limit_bytes=4 * 1024 * 1024),
        name="pack_tile",
    )(raw, obs_count)
    north = cycled(package, "lat", 1)
    south = cycled(package, "lat", -1)
    far_west = cycled(dipoles, "lon", 2)
    far_east = far_west if lon_tiles == 4 else cycled(dipoles, "lon", -2)
    west = cycled(package, "lon", 1)
    east = cycled(package, "lon", -1)
    north, south, far_west, far_east, west, east = lax.optimization_barrier((north, south, far_west, far_east, west, east))
    far_north = cycled(jnp.concatenate([north[:, slots:], west[:, slots:], east[:, slots:]], 1), "lat", 1)
    far_south = cycled(jnp.concatenate([south[:, slots:], west[:, slots:], east[:, slots:]], 1), "lat", -1)
    chunks = slots // CHUNK
    vmem = pl.BlockSpec(memory_space=pltpu.VMEM)

    def working(targets):
        return [
            pltpu.VMEM((5 * chunks, 8, CHUNK), jnp.float32),
            pltpu.VMEM((targets, 4, size, LANES), jnp.float32),
            pltpu.VMEM((targets, size, DEPTH), jnp.bfloat16),
            pltpu.VMEM((5 * chunks, DEPTH, CHUNK), jnp.bfloat16),
            pltpu.VMEM((5, size, 3 * CHUNK), jnp.bfloat16),
            pltpu.VMEM((5, size, 3 * CHUNK), jnp.bfloat16),
            pltpu.VMEM((3 * CHUNK, size), jnp.bfloat16),
            pltpu.VMEM((3 * CHUNK, size), jnp.bfloat16),
            pltpu.VMEM((5, size, CHUNK), jnp.float32),
            pltpu.VMEM((5, size, CHUNK), jnp.float32),
            pltpu.VMEM((2, 3, size, CHUNK), jnp.float32),
            pltpu.VMEM((3, 8, CHUNK), jnp.float32),
            pltpu.SMEM((5, 5), jnp.int32),
            pltpu.SMEM((2, 5 * chunks), jnp.int32),
            pltpu.SMEM((5,), jnp.int32),
            pltpu.SMEM((5,), jnp.int32),
        ]

    products = 2 * 3 * slots * size * size
    own_gram, own_right = pl.pallas_call(
        functools.partial(row_kernel, lat_tiles=lat_tiles, opening=True),
        out_shape=(
            jax.ShapeDtypeStruct((len(CROSS) + 1, size, size), jnp.float32),
            jax.ShapeDtypeStruct((size, LANES), jnp.float32),
        ),
        in_specs=[vmem] * 5,
        out_specs=(vmem, vmem),
        scratch_shapes=working(len(CROSS)),
        compiler_params=pltpu.CompilerParams(vmem_limit_bytes=26 * 1024 * 1024),
        cost_estimate=pl.CostEstimate(flops=5 * products, bytes_accessed=8 * size * size * 4, transcendentals=0),
        name="own_rows",
    )(package, north, south, west, east)
    gram, rhs = pl.pallas_call(
        functools.partial(row_kernel, lat_tiles=lat_tiles, opening=False),
        out_shape=(
            jax.ShapeDtypeStruct((len(OFFSETS), size, size), jnp.float32),
            jax.ShapeDtypeStruct((1, size), jnp.float32),
        ),
        in_specs=[vmem] * 11,
        out_specs=(pl.BlockSpec(memory_space=pl.ANY), vmem),
        scratch_shapes=working(len(OFFSETS))
        + [
            pltpu.VMEM((size, LANES), jnp.float32),
            pltpu.SMEM((len(OFFSETS),), jnp.int32),
            pltpu.VMEM((len(OFFSETS) + 1, size, size), jnp.float32),
            pltpu.SemaphoreType.DMA((len(OFFSETS),)),
        ],
        compiler_params=pltpu.CompilerParams(vmem_limit_bytes=44 * 1024 * 1024),
        cost_estimate=pl.CostEstimate(flops=20 * products, bytes_accessed=16 * size * size * 4, transcendentals=0),
        name="row_blocks",
    )(package, north, south, west, east, far_north, far_south, far_west, far_east, own_gram, own_right)
    return (gram[None, None], rhs[None])


def solution(mesh):
    in_specs = (
        P("lat", "lon", None, None),
        P("lat", "lon", None, None),
        P("lat", "lon", None, None),
        P("lat", "lon", None),
        P("lat", "lon"),
    )
    out_specs = (P("lat", "lon", None, None, None), P("lat", "lon", None))
    return jax.shard_map(shards, mesh=mesh, in_specs=in_specs, out_specs=out_specs, check_vma=False)
```

```python
import functools
import math

import jax
import jax.numpy as jnp
from jax import lax
from jax.experimental import pallas as pl
from jax.experimental.pallas import tpu as pltpu
from jax.sharding import PartitionSpec as P

CROSS = ((0, 0), (-1, 0), (1, 0), (0, -1), (0, 1))
OFFSETS = (
    (0, 0),
    (-1, 0),
    (1, 0),
    (0, -1),
    (0, 1),
    (-2, 0),
    (2, 0),
    (0, -2),
    (0, 2),
    (-1, -1),
    (-1, 1),
    (1, -1),
    (1, 1),
)
OBS_RADIUS = 1.06
SOURCE_RADIUS = 0.99
KERNEL_SCALE = 0.0001
HUBER_EDGE = 0.8
DEGREE = math.pi / 180.0
CHUNK = 512
ROWS = 16
WIDTH = 256
LANES = 128
DEPTH = 64
STRETCH = KERNEL_SCALE ** (-2.0 / 3.0)


def cycled(value, axis, steps):
    count = lax.axis_size(axis)
    return lax.ppermute(value, axis, [(i, (i + steps) % count) for i in range(count)])


def pack_kernel(raw, obs_count, package, dipoles, *, lat_tiles, lon_tiles):
    size = dipoles.shape[1]
    slots = raw.shape[1] - size
    obs_frac, obs_field = raw[0:2, :slots], raw[2:5, :slots]
    dipole_frac, moment = raw[0:2, slots:], raw[2:3, slots:]
    lat_index = lax.axis_index("lat").astype(jnp.float32)
    lon_index = lax.axis_index("lon").astype(jnp.float32)
    lat_span = 160.0 * DEGREE / lat_tiles
    lon_span = 2.0 * math.pi / lon_tiles

    def place(fraction, radius):
        row = lax.broadcasted_iota(jnp.int32, fraction.shape, 0)
        angle = jnp.where(row == 0, -80.0 * DEGREE + (lat_index + fraction) * lat_span, (lon_index + fraction) * lon_span)
        cosine, sine = jnp.cos(angle), jnp.sin(angle)
        return [
            radius * (cosine[0:1] * cosine[1:2]),
            radius * (cosine[0:1] * sine[1:2]),
            radius * sine[0:1],
        ]

    for row, value in enumerate(place(obs_frac, OBS_RADIUS)):
        package[row : row + 1, :slots] = value
    package[3:6, :slots] = obs_field
    index = lax.broadcasted_iota(jnp.int32, (1, slots), 1)
    package[6:7, :slots] = (index < obs_count[0, 0]).astype(jnp.float32)
    package[7:8, :slots] = jnp.zeros((1, slots), jnp.float32)
    rows = place(dipole_frac, SOURCE_RADIUS) + [moment, jnp.zeros((4, size), jnp.float32)]
    filled = jnp.concatenate(rows, 0)
    package[:, slots:] = filled
    dipoles[...] = filled


def split(values):
    high = values.astype(jnp.bfloat16).astype(jnp.float32)
    rest = values - high
    middle = rest.astype(jnp.bfloat16).astype(jnp.float32)
    return high, middle, rest - middle


def row_kernel(*refs, lat_tiles, opening):
    refs = list(refs)
    own_ref, north_ref, south_ref, west_ref, east_ref = refs[:5]
    if opening:
        gram, right, column, tall = refs[5:9]
        rest = refs[9:10] + [column, tall] + refs[10:]
        tiles, targets = (0,), range(len(CROSS))
    else:
        far_north_ref, far_south_ref, far_west_ref, far_east_ref = refs[5:9]
        gram_in, right_in, column_in, tall_in, gram_ref, rhs_ref = refs[9:15]
        rest = refs[15:]
        tiles, targets = (3, 4, 1, 2), range(len(OFFSETS))
    (
        obs,
        column,
        tall,
        flat,
        held_even,
        held_odd,
        weighted_even,
        weighted_odd,
        apart_even,
        apart_odd,
        kept,
        predicted,
        table,
        items,
        members,
        counts,
    ) = rest[:16]
    if not opening:
        right, waits, gram, sent = rest[16:]
    size = right.shape[0]
    chunks = obs.shape[0] // len(CROSS)
    slots = chunks * CHUNK
    lat = lax.axis_index("lat")

    arrived = (own_ref, north_ref, south_ref, west_ref, east_ref)
    for tile in tiles:
        for chunk in range(chunks):
            obs[tile * chunks + chunk] = arrived[tile][:, chunk * CHUNK : (chunk + 1) * CHUNK]
    sources = {offset: (ref, slots) for offset, ref in zip(CROSS, arrived)}
    if not opening:
        for at, offset in enumerate(((-2, 0), (-1, -1), (-1, 1))):
            sources[offset] = (far_north_ref, at * size)
        for at, offset in enumerate(((2, 0), (1, -1), (1, 1))):
            sources[offset] = (far_south_ref, at * size)
        sources[(0, -2)] = (far_west_ref, 0)
        sources[(0, 2)] = (far_east_ref, 0)

    def inside(step):
        return (lat + step >= 0) & (lat + step < lat_tiles)

    picks = lax.broadcasted_iota(jnp.int32, (DEPTH, 4 * LANES), 0)
    parts = lax.broadcasted_iota(jnp.int32, (DEPTH, 4 * LANES), 1) // LANES
    picks = ((picks == parts) | (picks == parts + 16) | (picks == parts + 32)).astype(jnp.bfloat16)
    row_of = lax.broadcasted_iota(jnp.int32, (8, size), 0)
    right[...] = jnp.zeros_like(right) if opening else right_in[...]
    for target in targets:
        if not opening and target < len(CROSS):
            gram[target] = gram_in[target]
            column[target] = column_in[target]
            tall[target] = tall_in[target]
            continue
        offset = OFFSETS[target]
        ref, start = sources[offset]
        values = ref[:, start : start + size]
        if offset[0] != 0:
            values = jnp.where((row_of < 3) | inside(offset[0]), values, 0.0)
        high, middle, low = split(values)
        ones = jnp.ones_like(values)
        stacked = jnp.concatenate([high, high, middle, high, low, middle, ones, jnp.zeros_like(values)], 0)
        upright = stacked.T.astype(jnp.bfloat16)
        gram[target] = jnp.zeros((size, size), jnp.float32)
        tall[target] = upright
        wide = lax.dot_general(upright, picks, (((1,), (0,)), ((), ())), preferred_element_type=jnp.float32)
        for part in range(4):
            column[target, part] = wide[:, part * LANES : (part + 1) * LANES]

    row_of = lax.broadcasted_iota(jnp.int32, (8, CHUNK), 0)
    base = STRETCH * (OBS_RADIUS * OBS_RADIUS + SOURCE_RADIUS * SOURCE_RADIUS)
    for at in [tile * chunks + chunk for tile in tiles for chunk in range(chunks)]:
        high, middle, low = split(jnp.where(row_of < 3, obs[at] * (-2.0 * STRETCH), 0.0))
        first, second, third = split(jnp.full((8, CHUNK), base, jnp.float32))
        constant = jnp.where(row_of == 0, first, jnp.where(row_of == 1, second, jnp.where(row_of == 2, third, 0.0)))
        stacked = jnp.concatenate([high, middle, high, low, high, middle, constant, jnp.zeros_like(high)], 0)
        flat[at] = stacked.astype(jnp.bfloat16)

    for tile in tiles:
        step = CROSS[tile]
        row = lat + step[0]
        first_row, last_row = row == 0, row == lat_tiles - 1
        own = (-step[0], -step[1])
        rest = [b for b in CROSS if b != own and b[0] == 0]
        ends = [b for b in CROSS if b != own and b[0] != 0]
        order = [OFFSETS.index((b[0] + step[0], b[1] + step[1])) for b in [own] + rest + ends]
        for at, target in enumerate(order):
            table[tile, at] = target
        if len(ends) == 2:
            table[tile, 3] = jnp.where(first_row, order[4], order[3])
            table[tile, 4] = jnp.where(first_row, order[3], order[4])
        members[tile] = 5 - first_row.astype(jnp.int32) - last_row.astype(jnp.int32)
        count = jnp.where(first_row | last_row, chunks, chunks // 2)
        counts[tile] = jnp.where(inside(step[0]), count, 0)

    total = jnp.int32(0)
    for full in (5, 4):
        for tile in tiles:

            def note(chunk, at, tile=tile):
                items[0, at] = tile
                items[1, at] = tile * chunks + chunk
                return at + 1

            total = lax.fori_loop(0, jnp.where(members[tile] == full, counts[tile], 0), note, total)


    def separate(tile, chunk, at, apart):
        apart[at] = lax.dot_general(
            tall[table[tile, at]], flat[chunk], (((1,), (0,)), ((), ())), preferred_element_type=jnp.float32
        )

    def evaluate(tile, chunk, at, held, apart):
        target = table[tile, at]
        spare = (at != 0).astype(jnp.int32)
        near = 1.5 * (OBS_RADIUS * OBS_RADIUS - SOURCE_RADIUS * SOURCE_RADIUS) * STRETCH
        for left in range(0, CHUNK, WIDTH):
            over = slice(left, left + WIDTH)
            point = [jnp.broadcast_to(obs[chunk, c : c + 1, over], (ROWS, WIDTH)) for c in range(3)]
            sums = [predicted[c, :, over] for c in range(3)]
            for start in range(0, size, ROWS):
                span = slice(start, start + ROWS)
                wide = [jnp.concatenate([column[target, part, span, :]] * (WIDTH // LANES), axis=1) for part in range(4)]
                inverse = lax.rsqrt(apart[at, span, over])
                inverse_square = inverse * inverse
                cube = inverse_square * inverse
                along = cube * (near * inverse_square - 1.5)
                across = along + cube
                for c in range(3):
                    value = along * point[c] - across * wide[c]
                    held[at, span, c * CHUNK + left : c * CHUNK + left + WIDTH] = value.astype(jnp.bfloat16)
                    kept[spare, c, span, over] = value
                    part = value * wide[3]
                    for sub in range(0, ROWS, 8):
                        sums[c] = sums[c] + part[sub : sub + 8]
            for c in range(3):
                predicted[c, :, over] = sums[c]

    def multiply(target, at, held, weighted):
        for half in (slice(0, size // 2), slice(size // 2, size)):
            gram[target, half] += lax.dot_general(
                held[at, half], weighted[...], (((1,), (0,)), ((), ())), preferred_element_type=jnp.float32
            )

    def flush(target):
        gram[target] = gram[target].T
        pltpu.make_async_copy(gram.at[target], gram_ref.at[target], sent.at[target]).start()

    def finish(chunk, weighted):
        present = obs[chunk, 6:7, :]
        scale, force = [], []
        for c in range(3):
            residual = obs[chunk, 3 + c : 4 + c, :] - jnp.sum(predicted[c], axis=0, keepdims=True)
            weight = present * HUBER_EDGE / jnp.maximum(jnp.abs(residual), HUBER_EDGE)
            scale.append(jnp.broadcast_to(weight, (ROWS, CHUNK)))
            force.append(jnp.broadcast_to(weight * residual, (ROWS, CHUNK)))
        for start in range(0, size, LANES):
            span = slice(start, start + LANES)
            for lane in range(0, CHUNK, LANES):
                over = slice(lane, lane + LANES)
                pull = right[span, :]
                for c in range(3):
                    value = kept[0, c, span, over]
                    scaled = (jnp.concatenate([scale[c][:, over]] * (LANES // ROWS), axis=0) * value).astype(jnp.bfloat16)
                    weighted[c * CHUNK + lane : c * CHUNK + lane + LANES, span] = scaled.T
                    pull = pull + jnp.concatenate([force[c][:, over]] * (LANES // ROWS), axis=0) * value
                right[span, :] = pull

    last = items[0, total - 1]
    twice = items[0, jnp.maximum(total - 2, 0)] == last

    if not opening:

        def clear(target, carry):
            waits[target] = 0
            return carry

        lax.fori_loop(0, len(OFFSETS), clear, 0)

        def mark(at, carry):
            waits[table[last, at]] = 1
            return carry

        lax.fori_loop(0, members[last], mark, 0)

    def early(target, carry):
        @pl.when(waits[target] == 0)
        def _():
            flush(target)

        return carry

    def advance(item, held, weighted, apart, held_before, weighted_before, apart_later):
        tile, chunk = items[0, item], items[1, item]
        before = items[0, jnp.maximum(item - 1, 0)]
        after = jnp.minimum(item + 1, total - 1)
        later, later_chunk = items[0, after], items[1, after]
        predicted[...] = jnp.zeros_like(predicted)

        if not opening:

            @pl.when((item == total - 1) & twice)
            def _():
                lax.fori_loop(0, len(OFFSETS), early, 0)

        def block(at, carry):
            separate(later, later_chunk, at, apart_later)
            target = jnp.where(item == 0, len(targets), table[before, at])
            multiply(target, at, held_before, weighted_before)
            evaluate(tile, chunk, at, held, apart)
            return carry

        lax.fori_loop(0, members[before], block, 0)
        finish(chunk, weighted)

    def pair(at, carry):
        advance(2 * at, held_even, weighted_even, apart_even, held_odd, weighted_odd, apart_odd)
        advance(2 * at + 1, held_odd, weighted_odd, apart_odd, held_even, weighted_even, apart_even)
        return carry

    def open_item(at, carry):
        separate(items[0, 0], items[1, 0], at, apart_even)
        return carry

    lax.fori_loop(0, members[items[0, 0]], open_item, 0)
    lax.fori_loop(0, total // 2, pair, 0)
    odd = total % 2 == 1

    @pl.when(odd)
    def _():
        advance(total - 1, held_even, weighted_even, apart_even, held_odd, weighted_odd, apart_odd)

    if not opening:

        @pl.when(jnp.logical_not(twice))
        def _():
            lax.fori_loop(0, len(OFFSETS), early, 0)

    def drain(held, weighted):
        def block(at, carry):
            if not opening:
                flush(table[last, at - 1])
            multiply(table[last, at], at, held, weighted)
            return carry

        multiply(table[last, 0], 0, held, weighted)
        lax.fori_loop(1, members[last], block, 0)
        if not opening:
            flush(table[last, members[last] - 1])

    @pl.when(odd)
    def _():
        drain(held_even, weighted_even)

    @pl.when(jnp.logical_not(odd))
    def _():
        drain(held_odd, weighted_odd)

    if not opening:
        rhs_ref[...] = jnp.sum(right[...].T, axis=0, keepdims=True)

        def close(target, carry):
            pltpu.make_async_copy(gram.at[target], gram_ref.at[target], sent.at[target]).wait()
            return carry

        lax.fori_loop(0, len(OFFSETS), close, 0)


def shards(obs_frac, obs_field, dipole_frac, dipole_moment, obs_count):
    lat_tiles = lax.axis_size("lat")
    lon_tiles = lax.axis_size("lon")
    size = dipole_frac.shape[3]
    slots = obs_frac.shape[3]
    observed = jnp.concatenate([obs_frac[0, 0], obs_field[0, 0], jnp.zeros((3, slots), jnp.float32)], 0)
    drawn = jnp.concatenate([dipole_frac[0, 0], dipole_moment[0], jnp.zeros((5, size), jnp.float32)], 0)
    raw = jnp.concatenate([observed, drawn], 1)
    package, dipoles = pl.pallas_call(
        functools.partial(pack_kernel, lat_tiles=lat_tiles, lon_tiles=lon_tiles),
        out_shape=(
            jax.ShapeDtypeStruct((8, slots + size), jnp.float32),
            jax.ShapeDtypeStruct((8, size), jnp.float32),
        ),
        in_specs=[pl.BlockSpec(memory_space=pltpu.VMEM), pl.BlockSpec(memory_space=pltpu.SMEM)],
        out_specs=(pl.BlockSpec(memory_space=pltpu.VMEM), pl.BlockSpec(memory_space=pltpu.VMEM)),
        compiler_params=pltpu.CompilerParams(vmem_limit_bytes=4 * 1024 * 1024),
        name="pack_tile",
    )(raw, obs_count)
    north = cycled(package, "lat", 1)
    south = cycled(package, "lat", -1)
    far_west = cycled(dipoles, "lon", 2)
    far_east = far_west if lon_tiles == 4 else cycled(dipoles, "lon", -2)
    west = cycled(package, "lon", 1)
    east = cycled(package, "lon", -1)
    north, south, far_west, far_east, west, east = lax.optimization_barrier((north, south, far_west, far_east, west, east))
    far_north = cycled(jnp.concatenate([north[:, slots:], west[:, slots:], east[:, slots:]], 1), "lat", 1)
    far_south = cycled(jnp.concatenate([south[:, slots:], west[:, slots:], east[:, slots:]], 1), "lat", -1)
    chunks = slots // CHUNK
    vmem = pl.BlockSpec(memory_space=pltpu.VMEM)

    def working(*dipole_room):
        return [
            pltpu.VMEM((5 * chunks, 8, CHUNK), jnp.float32),
            *dipole_room,
            pltpu.VMEM((5 * chunks, DEPTH, CHUNK), jnp.bfloat16),
            pltpu.VMEM((5, size, 3 * CHUNK), jnp.bfloat16),
            pltpu.VMEM((5, size, 3 * CHUNK), jnp.bfloat16),
            pltpu.VMEM((3 * CHUNK, size), jnp.bfloat16),
            pltpu.VMEM((3 * CHUNK, size), jnp.bfloat16),
            pltpu.VMEM((5, size, CHUNK), jnp.float32),
            pltpu.VMEM((5, size, CHUNK), jnp.float32),
            pltpu.VMEM((2, 3, size, CHUNK), jnp.float32),
            pltpu.VMEM((3, 8, CHUNK), jnp.float32),
            pltpu.SMEM((5, 5), jnp.int32),
            pltpu.SMEM((2, 5 * chunks), jnp.int32),
            pltpu.SMEM((5,), jnp.int32),
            pltpu.SMEM((5,), jnp.int32),
        ]

    products = 2 * 3 * slots * size * size
    handed = pl.pallas_call(
        functools.partial(row_kernel, lat_tiles=lat_tiles, opening=True),
        out_shape=(
            jax.ShapeDtypeStruct((len(CROSS) + 1, size, size), jnp.float32),
            jax.ShapeDtypeStruct((size, LANES), jnp.float32),
            jax.ShapeDtypeStruct((len(CROSS), 4, size, LANES), jnp.float32),
            jax.ShapeDtypeStruct((len(CROSS), size, DEPTH), jnp.bfloat16),
        ),
        in_specs=[vmem] * 5,
        out_specs=(vmem,) * 4,
        scratch_shapes=working(),
        compiler_params=pltpu.CompilerParams(vmem_limit_bytes=26 * 1024 * 1024),
        cost_estimate=pl.CostEstimate(flops=5 * products, bytes_accessed=8 * size * size * 4, transcendentals=0),
        name="own_rows",
    )(package, north, south, west, east)
    gram, rhs = pl.pallas_call(
        functools.partial(row_kernel, lat_tiles=lat_tiles, opening=False),
        out_shape=(
            jax.ShapeDtypeStruct((len(OFFSETS), size, size), jnp.float32),
            jax.ShapeDtypeStruct((1, size), jnp.float32),
        ),
        in_specs=[vmem] * 13,
        out_specs=(pl.BlockSpec(memory_space=pl.ANY), vmem),
        scratch_shapes=working(
            pltpu.VMEM((len(OFFSETS), 4, size, LANES), jnp.float32),
            pltpu.VMEM((len(OFFSETS), size, DEPTH), jnp.bfloat16),
        )
        + [
            pltpu.VMEM((size, LANES), jnp.float32),
            pltpu.SMEM((len(OFFSETS),), jnp.int32),
            pltpu.VMEM((len(OFFSETS) + 1, size, size), jnp.float32),
            pltpu.SemaphoreType.DMA((len(OFFSETS),)),
        ],
        compiler_params=pltpu.CompilerParams(vmem_limit_bytes=44 * 1024 * 1024),
        cost_estimate=pl.CostEstimate(flops=20 * products, bytes_accessed=16 * size * size * 4, transcendentals=0),
        name="row_blocks",
    )(package, north, south, west, east, far_north, far_south, far_west, far_east, *handed)
    return (gram[None, None], rhs[None])


def solution(mesh):
    in_specs = (
        P("lat", "lon", None, None),
        P("lat", "lon", None, None),
        P("lat", "lon", None, None),
        P("lat", "lon", None),
        P("lat", "lon"),
    )
    out_specs = (P("lat", "lon", None, None, None), P("lat", "lon", None))
    return jax.shard_map(shards, mesh=mesh, in_specs=in_specs, out_specs=out_specs, check_vma=False)
```

```python
import functools
import math

import jax
import jax.numpy as jnp
from jax import lax
from jax.experimental import pallas as pl
from jax.experimental.pallas import tpu as pltpu
from jax.sharding import PartitionSpec as P

CROSS = ((0, 0), (-1, 0), (1, 0), (0, -1), (0, 1))
OFFSETS = (
    (0, 0),
    (-1, 0),
    (1, 0),
    (0, -1),
    (0, 1),
    (-2, 0),
    (2, 0),
    (0, -2),
    (0, 2),
    (-1, -1),
    (-1, 1),
    (1, -1),
    (1, 1),
)
OBS_RADIUS = 1.06
SOURCE_RADIUS = 0.99
KERNEL_SCALE = 0.0001
HUBER_EDGE = 0.8
DEGREE = math.pi / 180.0
CHUNK = 512
ROWS = 16
WIDTH = 256
LANES = 128
DEPTH = 64
STRETCH = 1.0 / (1.5 * (OBS_RADIUS * OBS_RADIUS - SOURCE_RADIUS * SOURCE_RADIUS))
SHRINK = KERNEL_SCALE * STRETCH**1.5


def cycled(value, axis, steps):
    count = lax.axis_size(axis)
    return lax.ppermute(value, axis, [(i, (i + steps) % count) for i in range(count)])


def pack_kernel(raw, obs_count, package, dipoles, *, lat_tiles, lon_tiles):
    size = dipoles.shape[1]
    slots = raw.shape[1] - size
    obs_frac, obs_field = raw[0:2, :slots], raw[2:5, :slots]
    dipole_frac, moment = raw[0:2, slots:], raw[2:3, slots:]
    lat_index = lax.axis_index("lat").astype(jnp.float32)
    lon_index = lax.axis_index("lon").astype(jnp.float32)
    lat_span = 160.0 * DEGREE / lat_tiles
    lon_span = 2.0 * math.pi / lon_tiles

    def place(fraction, radius):
        row = lax.broadcasted_iota(jnp.int32, fraction.shape, 0)
        angle = jnp.where(row == 0, -80.0 * DEGREE + (lat_index + fraction) * lat_span, (lon_index + fraction) * lon_span)
        cosine, sine = jnp.cos(angle), jnp.sin(angle)
        return [
            radius * (cosine[0:1] * cosine[1:2]),
            radius * (cosine[0:1] * sine[1:2]),
            radius * sine[0:1],
        ]

    for row, value in enumerate(place(obs_frac, OBS_RADIUS)):
        package[row : row + 1, :slots] = value
    package[3:6, :slots] = obs_field
    index = lax.broadcasted_iota(jnp.int32, (1, slots), 1)
    package[6:7, :slots] = (index < obs_count[0, 0]).astype(jnp.float32)
    package[7:8, :slots] = jnp.zeros((1, slots), jnp.float32)
    rows = place(dipole_frac, SOURCE_RADIUS) + [moment, jnp.zeros((4, size), jnp.float32)]
    filled = jnp.concatenate(rows, 0)
    package[:, slots:] = filled
    dipoles[...] = filled


def split(values):
    high = values.astype(jnp.bfloat16).astype(jnp.float32)
    rest = values - high
    middle = rest.astype(jnp.bfloat16).astype(jnp.float32)
    return high, middle, rest - middle


def row_kernel(*refs, lat_tiles, opening):
    refs = list(refs)
    own_ref, north_ref, south_ref, west_ref, east_ref = refs[:5]
    if opening:
        gram, right, column, tall = refs[5:9]
        rest = refs[9:10] + [column, tall] + refs[10:]
        tiles, targets = (0,), range(len(CROSS))
    else:
        far_north_ref, far_south_ref, far_west_ref, far_east_ref = refs[5:9]
        gram_in, right_in, column_in, tall_in, gram_ref, rhs_ref = refs[9:15]
        rest = refs[15:]
        tiles, targets = (3, 4, 1, 2), range(len(OFFSETS))
    (
        obs,
        column,
        tall,
        flat,
        held_even,
        held_odd,
        weighted_even,
        weighted_odd,
        apart_even,
        apart_odd,
        kept,
        predicted,
        table,
        items,
        members,
        counts,
    ) = rest[:16]
    if not opening:
        right, waits, gram, sent = rest[16:]
    size = right.shape[0]
    chunks = obs.shape[0] // len(CROSS)
    slots = chunks * CHUNK
    lat = lax.axis_index("lat")

    arrived = (own_ref, north_ref, south_ref, west_ref, east_ref)
    for tile in tiles:
        for chunk in range(chunks):
            seen = arrived[tile][:, chunk * CHUNK : (chunk + 1) * CHUNK]
            place = lax.broadcasted_iota(jnp.int32, seen.shape, 0)
            obs[tile * chunks + chunk] = jnp.where(place < 3, seen * SHRINK, seen)
    sources = {offset: (ref, slots) for offset, ref in zip(CROSS, arrived)}
    if not opening:
        for at, offset in enumerate(((-2, 0), (-1, -1), (-1, 1))):
            sources[offset] = (far_north_ref, at * size)
        for at, offset in enumerate(((2, 0), (1, -1), (1, 1))):
            sources[offset] = (far_south_ref, at * size)
        sources[(0, -2)] = (far_west_ref, 0)
        sources[(0, 2)] = (far_east_ref, 0)

    def inside(step):
        return (lat + step >= 0) & (lat + step < lat_tiles)

    picks = lax.broadcasted_iota(jnp.int32, (DEPTH, 4 * LANES), 0)
    parts = lax.broadcasted_iota(jnp.int32, (DEPTH, 4 * LANES), 1) // LANES
    picks = ((picks == parts) | (picks == parts + 16) | (picks == parts + 32)).astype(jnp.bfloat16)
    row_of = lax.broadcasted_iota(jnp.int32, (8, size), 0)
    right[...] = jnp.zeros_like(right) if opening else right_in[...]
    for target in targets:
        if not opening and target < len(CROSS):
            gram[target] = gram_in[target]
            column[target] = column_in[target]
            tall[target] = tall_in[target]
            continue
        offset = OFFSETS[target]
        ref, start = sources[offset]
        values = ref[:, start : start + size]
        values = jnp.where(row_of < 3, values * SHRINK, values)
        if offset[0] != 0:
            values = jnp.where((row_of < 3) | inside(offset[0]), values, 0.0)
        high, middle, low = split(values)
        ones = jnp.ones_like(values)
        stacked = jnp.concatenate([high, high, middle, high, low, middle, ones, jnp.zeros_like(values)], 0)
        upright = stacked.T.astype(jnp.bfloat16)
        gram[target] = jnp.zeros((size, size), jnp.float32)
        tall[target] = upright
        wide = lax.dot_general(upright, picks, (((1,), (0,)), ((), ())), preferred_element_type=jnp.float32)
        for part in range(4):
            column[target, part] = wide[:, part * LANES : (part + 1) * LANES]

    row_of = lax.broadcasted_iota(jnp.int32, (8, CHUNK), 0)
    base = STRETCH * (OBS_RADIUS * OBS_RADIUS + SOURCE_RADIUS * SOURCE_RADIUS)
    for tile, chunk in [(tile, chunk) for tile in tiles for chunk in range(chunks)]:
        at = tile * chunks + chunk
        seen = arrived[tile][:, chunk * CHUNK : (chunk + 1) * CHUNK]
        high, middle, low = split(jnp.where(row_of < 3, seen * (-2.0 * STRETCH / SHRINK), 0.0))
        first, second, third = split(jnp.full((8, CHUNK), base, jnp.float32))
        constant = jnp.where(row_of == 0, first, jnp.where(row_of == 1, second, jnp.where(row_of == 2, third, 0.0)))
        stacked = jnp.concatenate([high, middle, high, low, high, middle, constant, jnp.zeros_like(high)], 0)
        flat[at] = stacked.astype(jnp.bfloat16)

    for tile in tiles:
        step = CROSS[tile]
        row = lat + step[0]
        first_row, last_row = row == 0, row == lat_tiles - 1
        own = (-step[0], -step[1])
        rest = [b for b in CROSS if b != own and b[0] == 0]
        ends = [b for b in CROSS if b != own and b[0] != 0]
        order = [OFFSETS.index((b[0] + step[0], b[1] + step[1])) for b in [own] + rest + ends]
        for at, target in enumerate(order):
            table[tile, at] = target
        if len(ends) == 2:
            table[tile, 3] = jnp.where(first_row, order[4], order[3])
            table[tile, 4] = jnp.where(first_row, order[3], order[4])
        members[tile] = 5 - first_row.astype(jnp.int32) - last_row.astype(jnp.int32)
        count = jnp.where(first_row | last_row, chunks, chunks // 2)
        counts[tile] = jnp.where(inside(step[0]), count, 0)

    total = jnp.int32(0)
    for full in (5, 4):
        for tile in tiles:

            def note(chunk, at, tile=tile):
                items[0, at] = tile
                items[1, at] = tile * chunks + chunk
                return at + 1

            total = lax.fori_loop(0, jnp.where(members[tile] == full, counts[tile], 0), note, total)


    def separate(tile, chunk, at, apart):
        apart[at] = lax.dot_general(
            tall[table[tile, at]], flat[chunk], (((1,), (0,)), ((), ())), preferred_element_type=jnp.float32
        )

    def evaluate(tile, chunk, at, held, apart):
        target = table[tile, at]
        spare = (at != 0).astype(jnp.int32)
        for left in range(0, CHUNK, WIDTH):
            over = slice(left, left + WIDTH)
            point = [jnp.broadcast_to(obs[chunk, c : c + 1, over], (ROWS, WIDTH)) for c in range(3)]
            sums = [predicted[c, :, over] for c in range(3)]
            for start in range(0, size, ROWS):
                span = slice(start, start + ROWS)
                wide = [jnp.concatenate([column[target, part, span, :]] * (WIDTH // LANES), axis=1) for part in range(4)]
                inverse = lax.rsqrt(apart[at, span, over])
                inverse_square = inverse * inverse
                cube = inverse_square * inverse
                along = cube * (inverse_square - 1.5)
                across = along + cube
                for c in range(3):
                    value = along * point[c] - across * wide[c]
                    held[at, span, c * CHUNK + left : c * CHUNK + left + WIDTH] = value.astype(jnp.bfloat16)
                    kept[spare, c, span, over] = value
                    part = value * wide[3]
                    for sub in range(0, ROWS, 8):
                        sums[c] = sums[c] + part[sub : sub + 8]
            for c in range(3):
                predicted[c, :, over] = sums[c]

    def multiply(target, at, held, weighted):
        for half in (slice(0, size // 2), slice(size // 2, size)):
            gram[target, half] += lax.dot_general(
                held[at, half], weighted[...], (((1,), (0,)), ((), ())), preferred_element_type=jnp.float32
            )

    def flush(target):
        gram[target] = gram[target].T
        pltpu.make_async_copy(gram.at[target], gram_ref.at[target], sent.at[target]).start()

    def finish(chunk, weighted):
        present = obs[chunk, 6:7, :]
        scale, force = [], []
        for c in range(3):
            residual = obs[chunk, 3 + c : 4 + c, :] - jnp.sum(predicted[c], axis=0, keepdims=True)
            weight = present * HUBER_EDGE / jnp.maximum(jnp.abs(residual), HUBER_EDGE)
            scale.append(jnp.broadcast_to(weight, (ROWS, CHUNK)))
            force.append(jnp.broadcast_to(weight * residual, (ROWS, CHUNK)))
        for start in range(0, size, LANES):
            span = slice(start, start + LANES)
            for lane in range(0, CHUNK, LANES):
                over = slice(lane, lane + LANES)
                pull = right[span, :]
                for c in range(3):
                    value = kept[0, c, span, over]
                    scaled = (jnp.concatenate([scale[c][:, over]] * (LANES // ROWS), axis=0) * value).astype(jnp.bfloat16)
                    weighted[c * CHUNK + lane : c * CHUNK + lane + LANES, span] = scaled.T
                    pull = pull + jnp.concatenate([force[c][:, over]] * (LANES // ROWS), axis=0) * value
                right[span, :] = pull

    last = items[0, total - 1]
    twice = items[0, jnp.maximum(total - 2, 0)] == last

    if not opening:

        def clear(target, carry):
            waits[target] = 0
            return carry

        lax.fori_loop(0, len(OFFSETS), clear, 0)

        def mark(at, carry):
            waits[table[last, at]] = 1
            return carry

        lax.fori_loop(0, members[last], mark, 0)

    def early(target, carry):
        @pl.when(waits[target] == 0)
        def _():
            flush(target)

        return carry

    def advance(item, held, weighted, apart, held_before, weighted_before, apart_later):
        tile, chunk = items[0, item], items[1, item]
        before = items[0, jnp.maximum(item - 1, 0)]
        after = jnp.minimum(item + 1, total - 1)
        later, later_chunk = items[0, after], items[1, after]
        predicted[...] = jnp.zeros_like(predicted)

        if not opening:

            @pl.when((item == total - 1) & twice)
            def _():
                lax.fori_loop(0, len(OFFSETS), early, 0)

        def block(at, carry):
            separate(later, later_chunk, at, apart_later)
            target = jnp.where(item == 0, len(targets), table[before, at])
            multiply(target, at, held_before, weighted_before)
            evaluate(tile, chunk, at, held, apart)
            return carry

        lax.fori_loop(0, members[before], block, 0)
        finish(chunk, weighted)

    def pair(at, carry):
        advance(2 * at, held_even, weighted_even, apart_even, held_odd, weighted_odd, apart_odd)
        advance(2 * at + 1, held_odd, weighted_odd, apart_odd, held_even, weighted_even, apart_even)
        return carry

    def open_item(at, carry):
        separate(items[0, 0], items[1, 0], at, apart_even)
        return carry

    lax.fori_loop(0, members[items[0, 0]], open_item, 0)
    lax.fori_loop(0, total // 2, pair, 0)
    odd = total % 2 == 1

    @pl.when(odd)
    def _():
        advance(total - 1, held_even, weighted_even, apart_even, held_odd, weighted_odd, apart_odd)

    if not opening:

        @pl.when(jnp.logical_not(twice))
        def _():
            lax.fori_loop(0, len(OFFSETS), early, 0)

    def drain(held, weighted):
        def block(at, carry):
            if not opening:
                flush(table[last, at - 1])
            multiply(table[last, at], at, held, weighted)
            return carry

        multiply(table[last, 0], 0, held, weighted)
        lax.fori_loop(1, members[last], block, 0)
        if not opening:
            flush(table[last, members[last] - 1])

    @pl.when(odd)
    def _():
        drain(held_even, weighted_even)

    @pl.when(jnp.logical_not(odd))
    def _():
        drain(held_odd, weighted_odd)

    if not opening:
        rhs_ref[...] = jnp.sum(right[...].T, axis=0, keepdims=True)

        def close(target, carry):
            pltpu.make_async_copy(gram.at[target], gram_ref.at[target], sent.at[target]).wait()
            return carry

        lax.fori_loop(0, len(OFFSETS), close, 0)


def shards(obs_frac, obs_field, dipole_frac, dipole_moment, obs_count):
    lat_tiles = lax.axis_size("lat")
    lon_tiles = lax.axis_size("lon")
    size = dipole_frac.shape[3]
    slots = obs_frac.shape[3]
    observed = jnp.concatenate([obs_frac[0, 0], obs_field[0, 0], jnp.zeros((3, slots), jnp.float32)], 0)
    drawn = jnp.concatenate([dipole_frac[0, 0], dipole_moment[0], jnp.zeros((5, size), jnp.float32)], 0)
    raw = jnp.concatenate([observed, drawn], 1)
    package, dipoles = pl.pallas_call(
        functools.partial(pack_kernel, lat_tiles=lat_tiles, lon_tiles=lon_tiles),
        out_shape=(
            jax.ShapeDtypeStruct((8, slots + size), jnp.float32),
            jax.ShapeDtypeStruct((8, size), jnp.float32),
        ),
        in_specs=[pl.BlockSpec(memory_space=pltpu.VMEM), pl.BlockSpec(memory_space=pltpu.SMEM)],
        out_specs=(pl.BlockSpec(memory_space=pltpu.VMEM), pl.BlockSpec(memory_space=pltpu.VMEM)),
        compiler_params=pltpu.CompilerParams(vmem_limit_bytes=4 * 1024 * 1024),
        name="pack_tile",
    )(raw, obs_count)
    north = cycled(package, "lat", 1)
    south = cycled(package, "lat", -1)
    far_west = cycled(dipoles, "lon", 2)
    far_east = far_west if lon_tiles == 4 else cycled(dipoles, "lon", -2)
    west = cycled(package, "lon", 1)
    east = cycled(package, "lon", -1)
    north, south, far_west, far_east, west, east = lax.optimization_barrier((north, south, far_west, far_east, west, east))
    far_north = cycled(jnp.concatenate([north[:, slots:], west[:, slots:], east[:, slots:]], 1), "lat", 1)
    far_south = cycled(jnp.concatenate([south[:, slots:], west[:, slots:], east[:, slots:]], 1), "lat", -1)
    chunks = slots // CHUNK
    vmem = pl.BlockSpec(memory_space=pltpu.VMEM)

    def working(*dipole_room):
        return [
            pltpu.VMEM((5 * chunks, 8, CHUNK), jnp.float32),
            *dipole_room,
            pltpu.VMEM((5 * chunks, DEPTH, CHUNK), jnp.bfloat16),
            pltpu.VMEM((5, size, 3 * CHUNK), jnp.bfloat16),
            pltpu.VMEM((5, size, 3 * CHUNK), jnp.bfloat16),
            pltpu.VMEM((3 * CHUNK, size), jnp.bfloat16),
            pltpu.VMEM((3 * CHUNK, size), jnp.bfloat16),
            pltpu.VMEM((5, size, CHUNK), jnp.float32),
            pltpu.VMEM((5, size, CHUNK), jnp.float32),
            pltpu.VMEM((2, 3, size, CHUNK), jnp.float32),
            pltpu.VMEM((3, 8, CHUNK), jnp.float32),
            pltpu.SMEM((5, 5), jnp.int32),
            pltpu.SMEM((2, 5 * chunks), jnp.int32),
            pltpu.SMEM((5,), jnp.int32),
            pltpu.SMEM((5,), jnp.int32),
        ]

    products = 2 * 3 * slots * size * size
    handed = pl.pallas_call(
        functools.partial(row_kernel, lat_tiles=lat_tiles, opening=True),
        out_shape=(
            jax.ShapeDtypeStruct((len(CROSS) + 1, size, size), jnp.float32),
            jax.ShapeDtypeStruct((size, LANES), jnp.float32),
            jax.ShapeDtypeStruct((len(CROSS), 4, size, LANES), jnp.float32),
            jax.ShapeDtypeStruct((len(CROSS), size, DEPTH), jnp.bfloat16),
        ),
        in_specs=[vmem] * 5,
        out_specs=(vmem,) * 4,
        scratch_shapes=working(),
        compiler_params=pltpu.CompilerParams(vmem_limit_bytes=26 * 1024 * 1024),
        cost_estimate=pl.CostEstimate(flops=5 * products, bytes_accessed=8 * size * size * 4, transcendentals=0),
        name="own_rows",
    )(package, north, south, west, east)
    gram, rhs = pl.pallas_call(
        functools.partial(row_kernel, lat_tiles=lat_tiles, opening=False),
        out_shape=(
            jax.ShapeDtypeStruct((len(OFFSETS), size, size), jnp.float32),
            jax.ShapeDtypeStruct((1, size), jnp.float32),
        ),
        in_specs=[vmem] * 13,
        out_specs=(pl.BlockSpec(memory_space=pl.ANY), vmem),
        scratch_shapes=working(
            pltpu.VMEM((len(OFFSETS), 4, size, LANES), jnp.float32),
            pltpu.VMEM((len(OFFSETS), size, DEPTH), jnp.bfloat16),
        )
        + [
            pltpu.VMEM((size, LANES), jnp.float32),
            pltpu.SMEM((len(OFFSETS),), jnp.int32),
            pltpu.VMEM((len(OFFSETS) + 1, size, size), jnp.float32),
            pltpu.SemaphoreType.DMA((len(OFFSETS),)),
        ],
        compiler_params=pltpu.CompilerParams(vmem_limit_bytes=44 * 1024 * 1024),
        cost_estimate=pl.CostEstimate(flops=20 * products, bytes_accessed=16 * size * size * 4, transcendentals=0),
        name="row_blocks",
    )(package, north, south, west, east, far_north, far_south, far_west, far_east, *handed)
    return (gram[None, None], rhs[None])


def solution(mesh):
    in_specs = (
        P("lat", "lon", None, None),
        P("lat", "lon", None, None),
        P("lat", "lon", None, None),
        P("lat", "lon", None),
        P("lat", "lon"),
    )
    out_specs = (P("lat", "lon", None, None, None), P("lat", "lon", None))
    return jax.shard_map(shards, mesh=mesh, in_specs=in_specs, out_specs=out_specs, check_vma=False)
```
